512 devices in a mesh: group: 16 (over x, z_hi), shard: 32 (over z_lo, y, core).
Axes of the slice: x: 4, y: 4, z: 16 (z_hi: 4, z_lo: 4; z = z_hi * 4 + z_lo), core: 2. Of those that a mesh axis runs over, the one named last changes fastest.
Arguments:
- step_count: int32 [1], replicated, may hold values from 2 to 8
- block_order: int32 [224], replicated, may hold values from 0 to 223, as said below
- saved_tiles: bfloat16 [512, 4, 18, 18, 256], P(('group', 'shard')), may hold values from -6 to 6
- pre_act: bfloat16 [262144, 256], P(('group', 'shard')), may hold values from -6 to 6
- grad_output: bfloat16 [262144, 256], P(('group', 'shard')), may hold values from -0.0234375 to 0.0234375
- pointwise_live: bfloat16 [256, 256], replicated, may hold values from -0.375 to 0.375
- master_rows: float32 [7168, 256], P('shard'), may hold values from -0.25 to 0.25, as said below
- row_moment: float32 [7168], P('shard'), may hold values from 0.5 to 30, as said below
- col_moment: float32 [2, 256], replicated, may hold values from 0.03 to 0.3
- next_tiles: bfloat16 [512, 4, 18, 18, 256], P(('group', 'shard')), may hold values from -6 to 6
Outputs:
- update_rows: float32 [7168, 256], P('shard')
- new_master: float32 [7168, 256], P('shard')
- new_row_moment: float32 [7168], P('shard')
- new_col_moment: float32 [2, 256], replicated
- next_output: bfloat16 [262144, 256], P(('group', 'shard'))
The draws below stay inside these ranges and needn't reach their ends.
Inputs may be any that keep to these rules, and one draw needn't show every extreme that they name: `block_order`: a permutation of 0 to 223. `master_rows`: rows of the 3x3x3 kernel are of order (6912) ** -0.5 and rows of the 1x1x1 kernel of order 256 ** -0.5. `row_moment`: positive row factors.
All inputs are finite; a program needn't handle non-finite values.
Results may differ from the reference program's by a relative error of at most 0.023.
Values may be sent and summed in bfloat16 or wider, within the bound.
A program may use at most 64 MiB of HBM per device.

```python
import math
import jax
import jax.numpy as jnp
from jax import lax

CI = 256
CO = 256
BLK = 32
FR = 2
HW = 16
NB3 = 216
NB = 224
ROWS_DEV = 512
N_GROUP = 16
N_SHARD = 32


def block_permutation(key):
    return jax.random.permutation(jax.random.fold_in(key, 17), NB).astype(jnp.int32)


def draw_block_order(key, part):
    return block_permutation(key)


def draw_master_rows(key, part):
    order = block_permutation(key)
    is_small = jnp.repeat(order >= NB3, BLK, total_repeat_length=NB * BLK)
    scale = jnp.where(is_small, CO ** (-0.5), (27 * CI) ** (-0.5)).astype(jnp.float32)
    noise_key = jax.random.fold_in(key, 29)
    values = jax.random.truncated_normal(noise_key, -4.0, 4.0, (NB * BLK, CO), jnp.float32)
    return values * scale[:, None]


def draw_row_moment(key, part):
    position = jnp.arange(NB * BLK, dtype=jnp.float32) / (NB * BLK - 1)
    jitter = jax.random.uniform(jax.random.fold_in(key, 41), (NB * BLK,), jnp.float32, -0.7, 0.0)
    spread = 2.3
    return (30.0 * jnp.exp(jitter - spread * position)).astype(jnp.float32)


def steps_of(key, extent, shards, least, high):
    loudness, own = 1.0, jax.random.fold_in(key, 6)
    for axis_at, shards_of in shards:
        draws = jnp.exp(jax.random.uniform(jax.random.fold_in(own, axis_at), (shards_of,), jnp.float32, least / len(shards), high / len(shards)))
        loudness = loudness * jnp.repeat(draws, extent[axis_at] // shards_of).reshape([-1 if axis == axis_at else 1 for axis in range(len(extent))])
    return loudness


def noise(stream_key, shape, scale, limit, cuts=(), kind=jnp.bfloat16):
    drawn = jax.random.normal(stream_key, shape, jnp.float32) * scale
    if len(cuts) > 0:
        drawn = steps_of(stream_key, shape, cuts, -0.22, 0.18) * drawn
    return jnp.clip(drawn, min=-limit, max=limit).astype(kind)


def setup_inputs(seed: int = 0) -> dict:
    arg_keys = jax.random.split(jax.random.key(seed), 11)
    return {
        "step_count": jax.random.randint(arg_keys[0], (1,), 2, 9).astype(jnp.int32),
        "block_order": draw_block_order(jax.random.fold_in(arg_keys[10], 71), 0),
        "saved_tiles": noise(arg_keys[2], (N_GROUP * N_SHARD, FR + 2, HW + 2, HW + 2, CI), 1.0, 6.0, ((0, 512),)),
        "pre_act": noise(arg_keys[3], (N_GROUP * N_SHARD * ROWS_DEV, CO), 1.0, 6.0, ((0, 512),)),
        "grad_output": noise(arg_keys[4], (N_GROUP * N_SHARD * ROWS_DEV, CO), (2.0 * (N_GROUP * N_SHARD * ROWS_DEV) ** -0.5), 0.0234375, ((0, 512),)),
        "pointwise_live": noise(arg_keys[5], (CO, CO), CO ** -0.5, 0.375),
        "master_rows": draw_master_rows(jax.random.fold_in(arg_keys[10], 71), 0),
        "row_moment": draw_row_moment(jax.random.fold_in(arg_keys[10], 71), 0),
        "col_moment": jnp.clip(jnp.exp(jax.random.uniform(arg_keys[8], (2, CO), jnp.float32, math.log(0.03), math.log(0.3))), 0.03, 0.3),
        "next_tiles": noise(arg_keys[9], (N_GROUP * N_SHARD, FR + 2, HW + 2, HW + 2, CI), 1.0, 6.0, ((0, 512),)),
    }


learn_rate = 0.002
decay_power = 0.8

def silu_slope(values):
    sigma = jax.nn.sigmoid(values)
    return sigma * (1.0 + values * (1.0 - sigma))

def tap_views(frames):
    views = []
    for frame_off in range(3):
        for row_off in range(3):
            for col_off in range(3):
                window = frames[frame_off:frame_off + FR, row_off:row_off + HW, col_off:col_off + HW, :]
                views.append(window.reshape(FR * HW * HW, CI))
    return views

def contract_rows(left, right):
    return lax.dot_general(left, right, (((0,), (0,)), ((), ())), preferred_element_type=jnp.float32)

def kernel_sums(values, is_small):
    large_part = lax.optimization_barrier(jnp.sum(jnp.where(is_small[:, None], 0.0, values), axis=0))
    small_part = lax.optimization_barrier(jnp.sum(jnp.where(is_small[:, None], values, 0.0), axis=0))
    return jnp.stack([large_part, small_part])

def device_term(frames, pre_rows, grad_rows, pointwise_live):
    pre_float = pre_rows.astype(jnp.float32)
    activation = jax.nn.silu(pre_float).astype(jnp.bfloat16)
    grad_act = lax.dot_general(grad_rows, pointwise_live, (((1,), (1,)), ((), ())), preferred_element_type=jnp.float32)
    grad_pre = (grad_act * silu_slope(pre_float)).astype(jnp.bfloat16)
    pieces = [contract_rows(view, grad_pre) for view in tap_views(frames)]
    pieces.append(contract_rows(activation, grad_rows))
    return jnp.concatenate(pieces, axis=0).astype(jnp.bfloat16)

def forward_tile(frames, spatial, pointwise):
    hidden_sum = jnp.zeros((FR * HW * HW, CO), jnp.float32)
    for index_tap, view in enumerate(tap_views(frames)):
        hidden_sum = hidden_sum + jnp.dot(view, spatial[index_tap], preferred_element_type=jnp.float32)
    hidden_act = jax.nn.silu(hidden_sum).astype(jnp.bfloat16)
    return jnp.dot(hidden_act, pointwise, preferred_element_type=jnp.float32).astype(jnp.bfloat16)

def reference(step_count, block_order, saved_tiles, pre_act, grad_output, pointwise_live, master_rows, row_moment, col_moment, next_tiles):
    device_count = N_GROUP * N_SHARD
    total_rows = NB * BLK
    pre_all = pre_act.reshape(device_count, FR * HW * HW, CO)
    grad_all = grad_output.reshape(device_count, FR * HW * HW, CO)

    def accumulate(total, inputs):
        frames, pre_rows, grad_rows = inputs
        term = device_term(frames, pre_rows, grad_rows, pointwise_live)
        return (total + term.astype(jnp.float32), None)
    natural_grad, unused = lax.scan(accumulate, jnp.zeros((total_rows, CO), jnp.float32), (saved_tiles, pre_all, grad_all))
    gradient = jnp.take(natural_grad.reshape(NB, BLK, CO), block_order, axis=0).reshape(total_rows, CO)
    is_small = jnp.repeat(block_order >= NB3, BLK, total_repeat_length=total_rows)
    decay_rate = 1.0 - step_count.astype(jnp.float32)[0] ** (-decay_power)
    counts = jnp.array([27 * CI, CO], jnp.float32)
    squares = gradient * gradient
    new_row = decay_rate * row_moment + (1.0 - decay_rate) * lax.optimization_barrier(jnp.mean(squares, axis=1))
    col_total = kernel_sums(squares, is_small)
    new_col = decay_rate * col_moment + (1.0 - decay_rate) * col_total / counts[:, None]
    row_mean = kernel_sums(new_row[:, None], is_small)[:, 0] / counts
    col_rows = jnp.where(is_small[:, None], new_col[1], new_col[0])
    mean_rows = jnp.where(is_small, row_mean[1], row_mean[0])
    scaled = gradient / jnp.sqrt(new_row[:, None] * col_rows / mean_rows[:, None])
    square_total = kernel_sums(lax.optimization_barrier(jnp.sum(scaled * scaled, axis=1))[:, None], is_small)[:, 0]
    clip_factor = jnp.maximum(1.0, jnp.sqrt(square_total / (counts * CO)))
    update_rows = scaled / jnp.where(is_small, clip_factor[1], clip_factor[0])[:, None]
    new_master = master_rows - learn_rate * update_rows
    weights_low = new_master.astype(jnp.bfloat16)
    inverse = jnp.zeros((NB,), jnp.int32).at[block_order].set(jnp.arange(NB, dtype=jnp.int32))
    natural = jnp.take(weights_low.reshape(NB, BLK, CO), inverse, axis=0).reshape(total_rows, CO)
    spatial = natural[:27 * CI].reshape(27, CI, CO)
    pointwise = natural[27 * CI:]

    def forward_one(frames):
        return forward_tile(frames, spatial, pointwise)
    next_output = lax.map(forward_one, next_tiles).reshape(device_count * FR * HW * HW, CO)
    return (update_rows, new_master, new_row, new_col, next_output)
```

```python
import jax
import jax.numpy as jnp
from jax import lax
from jax.experimental import pallas as pl
from jax.experimental.pallas import tpu as pltpu
from jax.sharding import PartitionSpec as P

CI = 256
CO = 256
BLK = 32
FR = 2
HW = 16
NB3 = 216
NB = 224
OWN = 7
LARGE = 27.0 * CI
SMALL = 1.0 * CI

learn_rate = 0.002
decay_power = 0.8

MESH = pl.DeviceIdType.MESH


def silu_slope(values):
    sigma = jax.nn.sigmoid(values)
    return sigma * (1.0 + values * (1.0 - sigma))


def tap_views(frames):
    views = []
    for frame_off in range(3):
        for row_off in range(3):
            for col_off in range(3):
                window = frames[
                    frame_off : frame_off + FR, row_off : row_off + HW, col_off : col_off + HW, :
                ]
                views.append(window.reshape(FR * HW * HW, CI))
    return views


def contract_rows(left, right):
    return lax.dot_general(
        left, right, (((0,), (0,)), ((), ())), preferred_element_type=jnp.float32
    )


def step_kernel(
    term,
    aux,
    row_in,
    master,
    update,
    new_master,
    new_row,
    new_col,
    weights,
    core_in,
    y_sum,
    y_half,
    y_full,
    x_sum,
    x_half,
    x_full,
    z_sum,
    z_in,
    h_in,
    grad,
    stat_own,
    stat_core,
    stat_y,
    stat_z,
    send_sem,
    recv_sem,
):
    group = lax.axis_index("group")
    shard = lax.axis_index("shard")
    x = group // 4
    zh = group % 4
    c = shard % 2
    y = (shard // 2) % 4
    zl = shard // 8

    def dev_core():
        return (group, shard + 1 - 2 * c)

    def dev_y(d):
        return (group, zl * 8 + ((y + d) % 4) * 2 + c)

    def dev_z(d):
        return (group, ((zl + d) % 4) * 8 + y * 2 + c)

    def dev_x(d):
        return (((x + d) % 4) * 4 + zh, shard)

    def dev_h(d):
        return (x * 4 + (zh + d) % 4, shard)

    partners = [dev_core()]
    partners += [dev_y(d) for d in (1, 2, 3)]
    partners += [dev_x(d) for d in (1, 3)]
    partners += [dev_z(d) for d in (1, 2, 3)]
    partners += [dev_h(d) for d in (1, 2, 3)]
    barrier = pltpu.get_barrier_semaphore()
    for partner in partners:
        pl.semaphore_signal(barrier, inc=1, device_id=partner, device_id_type=MESH)
    pl.semaphore_wait(barrier, len(partners))

    started = []

    def send(src, dst, device):
        slot = len(started)
        copy = pltpu.make_async_remote_copy(
            src_ref=src,
            dst_ref=dst,
            send_sem=send_sem.at[slot],
            recv_sem=recv_sem.at[slot],
            device_id=device,
            device_id_type=MESH,
        )
        copy.start()
        started.append(copy)
        return copy

    f32 = jnp.float32
    bf16 = jnp.bfloat16

    def add_into(dst, count, reads):
        @pl.loop(0, count)
        def _(step):
            total = reads[0](step).astype(f32)
            for read in reads[1:]:
                total = total + read(step).astype(f32)
            dst(step, total.astype(bf16))

    core_copies = {}
    for d in (2, 1, 3, 0):
        j = (y + d) % 4
        core_copies[d] = send(term.at[1 - c, j], core_in.at[j], dev_core())

    def y_part(d, start, count, more=()):
        j = (y + d) % 4

        def put(step, value):
            y_sum[d, start + step // 4, step % 4] = value

        reads = [
            lambda step: term[c, j, start + step // 4, step % 4],
            lambda step: core_in[j, start + step // 4, step % 4],
        ]
        for slot in more:
            reads.append(lambda step, slot=slot: y_half[slot, step // 4, step % 4])
        add_into(put, 4 * count, reads)

    core_copies[2].wait_recv()
    y_part(2, 0, 2)
    half_0 = send(y_sum.at[2, pl.ds(0, 2)], y_half.at[0], dev_y(1))
    y_part(2, 2, 2)
    half_1 = send(y_sum.at[2, pl.ds(2, 2)], y_half.at[1], dev_y(3))
    core_copies[1].wait_recv()
    y_part(1, 2, 2)
    full_0b = send(y_sum.at[1, pl.ds(2, 2)], y_full.at[0, pl.ds(2, 2)], dev_y(1))
    core_copies[3].wait_recv()
    y_part(3, 0, 2)
    full_1a = send(y_sum.at[3, pl.ds(0, 2)], y_full.at[1, pl.ds(0, 2)], dev_y(3))
    half_0.wait_recv()
    y_part(1, 0, 2, more=(0,))
    full_0a = send(y_sum.at[1, pl.ds(0, 2)], y_full.at[0, pl.ds(0, 2)], dev_y(1))
    half_1.wait_recv()
    y_part(3, 2, 2, more=(1,))
    full_1b = send(y_sum.at[3, pl.ds(2, 2)], y_full.at[1, pl.ds(2, 2)], dev_y(3))
    core_copies[0].wait_recv()
    for copy in (full_0b, full_1a, full_0a, full_1b):
        copy.wait_recv()

    def x_part(d, start, count, more=()):
        q = (x + d) % 4

        def put(step, value):
            x_sum[d, start + step] = value

        reads = [
            lambda step: term[c, y, q, start + step],
            lambda step: core_in[y, q, start + step],
            lambda step: y_full[0, q, start + step],
            lambda step: y_full[1, q, start + step],
        ]
        for slot in more:
            reads.append(lambda step, slot=slot: x_half[slot, step])
        add_into(put, count, reads)

    x_part(2, 0, 2)
    half_0 = send(x_sum.at[2, pl.ds(0, 2)], x_half.at[0], dev_x(1))
    x_part(2, 2, 2)
    half_1 = send(x_sum.at[2, pl.ds(2, 2)], x_half.at[1], dev_x(3))
    x_part(1, 2, 2)
    full_0b = send(x_sum.at[1, pl.ds(2, 2)], x_full.at[0, pl.ds(2, 2)], dev_x(1))
    x_part(3, 0, 2)
    full_1a = send(x_sum.at[3, pl.ds(0, 2)], x_full.at[1, pl.ds(0, 2)], dev_x(3))
    half_0.wait_recv()
    x_part(1, 0, 2, more=(0,))
    full_0a = send(x_sum.at[1, pl.ds(0, 2)], x_full.at[0, pl.ds(0, 2)], dev_x(1))
    half_1.wait_recv()
    x_part(3, 2, 2, more=(1,))
    full_1b = send(x_sum.at[3, pl.ds(2, 2)], x_full.at[1, pl.ds(2, 2)], dev_x(3))
    x_part(0, 0, 4)
    for copy in (full_0b, full_1a, full_0a, full_1b):
        copy.wait_recv()

    z_copies = []
    for d in (3, 2, 1, 0):
        z = (zl + d) % 4
        z_sum[d] = (
            x_sum[0, z].astype(f32) + x_full[0, z].astype(f32) + x_full[1, z].astype(f32)
        ).astype(bf16)
        if d:
            z_copies.append(send(z_sum.at[d], z_in.at[d - 1], dev_z(d)))
    for copy in z_copies:
        copy.wait_recv()
    h_in[zh] = (
        (z_sum[0].astype(f32) + z_in[0].astype(f32))
        + (z_in[1].astype(f32) + z_in[2].astype(f32))
    ).astype(bf16)

    h_copies = [send(h_in.at[zh], h_in.at[zh], dev_h(d)) for d in (2, 1, 3)]
    for copy in h_copies:
        copy.wait_recv()
    grad[x] = (
        (h_in[0].astype(f32) + h_in[1].astype(f32)) + (h_in[2].astype(f32) + h_in[3].astype(f32))
    ).astype(bf16)

    left = (x + 3) % 4
    right = (x + 1) % 4
    to_right = send(grad.at[x], grad.at[x], dev_x(1))
    to_left = send(grad.at[x], grad.at[x], dev_x(3))
    to_right.wait_recv()
    on_right = send(grad.at[left, pl.ds(0, 4)], grad.at[left, pl.ds(0, 4)], dev_x(1))
    to_left.wait_recv()
    on_left = send(grad.at[right, pl.ds(4, 3)], grad.at[right, pl.ds(4, 3)], dev_x(3))
    on_right.wait_recv()
    on_left.wait_recv()

    decay = aux[0:1, :]
    decay_row = aux[0:1, 0:1]
    zero = jnp.zeros((1, 128), f32)
    zero_row = jnp.zeros((1, 1), f32)
    cols = [[zero, zero], [zero, zero]]
    mixed = [[zero, zero], [zero, zero]]
    rows = [zero_row, zero_row]
    for i in range(OWN):
        small = aux[8 + i : 9 + i, 0:128]
        is_kernel = (1.0 - small, small)
        for half in range(2):
            span = slice(16 * half, 16 * half + 16)
            squares = []
            for side in range(2):
                value = grad[2 * half + side, i].astype(f32)
                squares.append(value * value)
            mean = jnp.sum(squares[0] + squares[1], axis=1, keepdims=True) * (1.0 / CO)
            moment = decay_row * row_in[i, span, :] + (1.0 - decay_row) * mean
            new_row[i, span, :] = moment
            inverse = 1.0 / moment
            row_sum = jnp.sum(moment, axis=0, keepdims=True)
            for k in range(2):
                rows[k] = rows[k] + is_kernel[k][:, 0:1] * row_sum
            for side in range(2):
                plain = jnp.sum(squares[side], axis=0, keepdims=True)
                weighted = jnp.sum(squares[side] * inverse, axis=0, keepdims=True)
                for k in range(2):
                    cols[k][side] = cols[k][side] + is_kernel[k] * plain
                    mixed[k][side] = mixed[k][side] + is_kernel[k] * weighted
    for side in range(2):
        lanes = slice(128 * side, 128 * side + 128)
        for k in range(2):
            stat_own[k : k + 1, lanes] = cols[k][side]
            stat_own[2 + k : 3 + k, lanes] = mixed[k][side]
            stat_own[4 + k : 5 + k, lanes] = jnp.broadcast_to(rows[k], (1, 128))
        stat_own[6:8, lanes] = jnp.zeros((2, 128), f32)

    send(stat_own, stat_core, dev_core()).wait_recv()
    stat_y[y] = stat_own[...] + stat_core[...]
    y_copies = [send(stat_y.at[y], stat_y.at[y], dev_y(d)) for d in (2, 1, 3)]
    for copy in y_copies:
        copy.wait_recv()
    stat_z[zl] = (stat_y[0] + stat_y[1]) + (stat_y[2] + stat_y[3])
    z_copies = [send(stat_z.at[zl], stat_z.at[zl], dev_z(d)) for d in (3, 2, 1)]
    for copy in z_copies:
        copy.wait_recv()
    total = (stat_z[0] + stat_z[1]) + (stat_z[2] + stat_z[3])

    factors = []
    for k, rows_k in ((0, LARGE), (1, SMALL)):
        column = decay * aux[1 + k : 2 + k, :] + (1.0 - decay) * total[k : k + 1, :] / rows_k
        new_col[k : k + 1, :] = column
        row_mean = total[4 + k : 5 + k, 0:1] / rows_k
        square = row_mean * jnp.sum(total[2 + k : 3 + k, :] / column, axis=1, keepdims=True)
        clip = jnp.maximum(1.0, jnp.sqrt(square / (rows_k * CO)))
        factors.append(1.0 / (jnp.sqrt(column / row_mean) * clip))
    new_col[2:8, :] = jnp.zeros((6, 256), f32)

    for i in range(OWN):
        small = aux[8 + i : 9 + i, :]
        factor = (1.0 - small) * factors[0] + small * factors[1]
        for half in range(2):
            span = slice(16 * half, 16 * half + 16)
            scale = 1.0 / jnp.sqrt(new_row[i, span, :])
            for side in range(2):
                lanes = slice(128 * side, 128 * side + 128)
                value = grad[2 * half + side, i].astype(f32)
                change = value * scale * factor[:, lanes]
                update[i, span, lanes] = change
                fresh = master[i, span, lanes] - learn_rate * change
                new_master[i, span, lanes] = fresh
                quarter = 2 * half + side

                @pl.when(x == quarter)
                def _(fresh=fresh, quarter=quarter, i=i):
                    weights[c, y, quarter, zl, i] = fresh.astype(bf16)

    z_copies = [
        send(weights.at[c, y, x, zl], weights.at[c, y, x, zl], dev_z(d)) for d in (3, 2, 1)
    ]
    for copy in z_copies:
        copy.wait_recv()
    to_right = send(weights.at[c, y, x], weights.at[c, y, x], dev_x(1))
    to_left = send(weights.at[c, y, x], weights.at[c, y, x], dev_x(3))
    to_right.wait_recv()
    low, high = pl.ds(0, 2), pl.ds(2, 2)
    on_right = send(weights.at[c, y, left, low], weights.at[c, y, left, low], dev_x(1))
    to_left.wait_recv()
    on_left = send(weights.at[c, y, right, high], weights.at[c, y, right, high], dev_x(3))
    on_right.wait_recv()
    on_left.wait_recv()
    below = (y + 3) % 4
    above = (y + 1) % 4
    across = (y + 2) % 4
    to_above = send(weights.at[c, y], weights.at[c, y], dev_y(1))
    to_below = send(weights.at[c, y], weights.at[c, y], dev_y(3))
    cores = [send(weights.at[c, y], weights.at[c, y], dev_core())]
    to_above.wait_recv()
    on_above = send(weights.at[c, below, low], weights.at[c, below, low], dev_y(1))
    cores.append(send(weights.at[c, below], weights.at[c, below], dev_core()))
    to_below.wait_recv()
    on_below = send(weights.at[c, above, high], weights.at[c, above, high], dev_y(3))
    cores.append(send(weights.at[c, above], weights.at[c, above], dev_core()))
    on_above.wait_recv()
    cores.append(send(weights.at[c, across, low], weights.at[c, across, low], dev_core()))
    on_below.wait_recv()
    cores.append(send(weights.at[c, across, high], weights.at[c, across, high], dev_core()))
    for copy in cores:
        copy.wait_recv()
    assert len(started) == N_COPIES
    for copy in started:
        copy.wait_send()


N_COPIES = 49


def optimizer_step(term, aux, row_in, master):
    f32 = jnp.float32
    bf16 = jnp.bfloat16
    tile = (OWN, 16, 128)
    vmem = pl.BlockSpec(memory_space=pltpu.VMEM)
    return pl.pallas_call(
        step_kernel,
        name="optimizer_step",
        out_shape=(
            jax.ShapeDtypeStruct((OWN, 32, 256), f32),
            jax.ShapeDtypeStruct((OWN, 32, 256), f32),
            jax.ShapeDtypeStruct((OWN, 32, 1), f32),
            jax.ShapeDtypeStruct((8, 256), f32),
            jax.ShapeDtypeStruct((2, 4, 4, 4) + tile, bf16),
        ),
        in_specs=[vmem] * 4,
        out_specs=[vmem] * 5,
        scratch_shapes=[
            pltpu.VMEM((4, 4, 4) + tile, bf16),
            pltpu.VMEM((4, 4, 4) + tile, bf16),
            pltpu.VMEM((2, 2, 4) + tile, bf16),
            pltpu.VMEM((2, 4, 4) + tile, bf16),
            pltpu.VMEM((4, 4) + tile, bf16),
            pltpu.VMEM((2, 2) + tile, bf16),
            pltpu.VMEM((2, 4) + tile, bf16),
            pltpu.VMEM((4,) + tile, bf16),
            pltpu.VMEM((3,) + tile, bf16),
            pltpu.VMEM((4,) + tile, bf16),
            pltpu.VMEM((4,) + tile, bf16),
            pltpu.VMEM((8, 256), f32),
            pltpu.VMEM((8, 256), f32),
            pltpu.VMEM((4, 8, 256), f32),
            pltpu.VMEM((4, 8, 256), f32),
            pltpu.SemaphoreType.DMA((N_COPIES,)),
            pltpu.SemaphoreType.DMA((N_COPIES,)),
        ],
        compiler_params=pltpu.CompilerParams(collective_id=0, has_side_effects=True),
    )(term, aux, row_in, master)


def shards(
    step_count,
    block_order,
    saved_tiles,
    pre_act,
    grad_output,
    pointwise_live,
    master_rows,
    row_moment,
    col_moment,
    next_tiles,
):
    pre_float = pre_act.astype(jnp.float32)
    activation = jax.nn.silu(pre_float).astype(jnp.bfloat16)
    grad_act = lax.dot_general(
        grad_output, pointwise_live, (((1,), (1,)), ((), ())), preferred_element_type=jnp.float32
    )
    grad_pre = (grad_act * silu_slope(pre_float)).astype(jnp.bfloat16)
    pieces = [contract_rows(view, grad_pre) for view in tap_views(saved_tiles[0])]
    pieces.append(contract_rows(activation, grad_output))
    own_term = jnp.concatenate(pieces, axis=0).astype(jnp.bfloat16)
    total_rows = NB * BLK
    order = block_order.reshape(4, 4, 2, OWN).transpose(2, 1, 0, 3)
    quarters = jnp.arange(4, dtype=jnp.int32)[None, None, :, None, None]
    source = order[:, :, None] * 4 + quarters
    tiles = own_term.reshape(NB, 2, 16, 2, 128).transpose(0, 1, 3, 2, 4).reshape(NB * 4, 16, 128)
    term = jnp.take(tiles, source.reshape(-1), axis=0).reshape(2, 4, 4, 4, OWN, 16, 128)

    owner = lax.axis_index("shard")
    own_blocks = lax.dynamic_slice_in_dim(block_order, owner * OWN, OWN)
    is_small = (own_blocks >= NB3).astype(jnp.float32)
    decay_rate = 1.0 - step_count.astype(jnp.float32)[0] ** (-decay_power)
    aux = jnp.concatenate(
        [
            jnp.broadcast_to(decay_rate, (1, CO)),
            col_moment,
            jnp.zeros((5, CO), jnp.float32),
            jnp.broadcast_to(is_small[:, None], (OWN, CO)),
            jnp.zeros((1, CO), jnp.float32),
        ],
        axis=0,
    )
    update, new_master, new_row, new_col, gathered = optimizer_step(
        term, aux, row_moment.reshape(OWN, BLK, 1), master_rows.reshape(OWN, BLK, CO)
    )
    position = jnp.zeros((NB,), jnp.int32).at[order.reshape(-1)].set(jnp.arange(NB, dtype=jnp.int32))
    outer, inner = position // 28, position % 28
    place = outer[:, None] * 112 + jnp.arange(4, dtype=jnp.int32)[None, :] * 28 + inner[:, None]
    natural = jnp.take(gathered.reshape(NB * 4, 16, 128), place.reshape(-1), axis=0)
    natural = natural.reshape(NB, 2, 2, 16, 128).transpose(0, 1, 3, 2, 4).reshape(total_rows, CO)
    spatial = natural[: 27 * CI].reshape(27, CI, CO)
    pointwise = natural[27 * CI :]
    hidden_sum = jnp.zeros((FR * HW * HW, CO), jnp.float32)
    for index_tap, view in enumerate(tap_views(next_tiles[0])):
        hidden_sum = hidden_sum + jnp.dot(
            view, spatial[index_tap], preferred_element_type=jnp.float32
        )
    hidden_act = jax.nn.silu(hidden_sum).astype(jnp.bfloat16)
    next_output = jnp.dot(hidden_act, pointwise, preferred_element_type=jnp.float32).astype(
        jnp.bfloat16
    )
    return (
        update.reshape(master_rows.shape),
        new_master.reshape(master_rows.shape),
        new_row.reshape(row_moment.shape),
        new_col[:2],
        next_output,
    )


def solution(mesh):
    in_specs = (
        P(),
        P(),
        P(("group", "shard"), None, None, None, None),
        P(("group", "shard"), None),
        P(("group", "shard"), None),
        P(),
        P("shard", None),
        P("shard"),
        P(),
        P(("group", "shard"), None, None, None, None),
    )
    out_specs = (P("shard", None), P("shard", None), P("shard"), P(), P(("group", "shard"), None))
    return jax.shard_map(shards, mesh=mesh, in_specs=in_specs, out_specs=out_specs, check_vma=False)
```

```python
import jax
import jax.numpy as jnp
from jax import lax
from jax.experimental import pallas as pl
from jax.experimental.pallas import tpu as pltpu
from jax.sharding import PartitionSpec as P

CI = 256
CO = 256
BLK = 32
FR = 2
HW = 16
NB3 = 216
NB = 224
OWN = 7
LARGE = 27.0 * CI
SMALL = 1.0 * CI

learn_rate = 0.002
decay_power = 0.8

MESH = pl.DeviceIdType.MESH


def step_kernel(
    term,
    aux,
    row_in,
    master,
    update,
    new_master,
    new_row,
    new_col,
    weights,
    core_in,
    y_sum,
    y_half,
    y_full,
    x_sum,
    x_half,
    x_full,
    z_sum,
    z_in,
    h_in,
    grad,
    stat_own,
    stat_core,
    stat_y,
    stat_z,
    send_sem,
    recv_sem,
):
    group = lax.axis_index("group")
    shard = lax.axis_index("shard")
    x = group // 4
    zh = group % 4
    c = shard % 2
    y = (shard // 2) % 4
    zl = shard // 8

    def dev_core():
        return (group, shard + 1 - 2 * c)

    def dev_y(d):
        return (group, zl * 8 + ((y + d) % 4) * 2 + c)

    def dev_z(d):
        return (group, ((zl + d) % 4) * 8 + y * 2 + c)

    def dev_x(d):
        return (((x + d) % 4) * 4 + zh, shard)

    def dev_h(d):
        return (x * 4 + (zh + d) % 4, shard)

    partners = [dev_core()]
    partners += [dev_y(d) for d in (1, 2, 3)]
    partners += [dev_x(d) for d in (1, 3)]
    partners += [dev_z(d) for d in (1, 2, 3)]
    partners += [dev_h(d) for d in (1, 2, 3)]
    barrier = pltpu.get_barrier_semaphore()
    for partner in partners:
        pl.semaphore_signal(barrier, inc=1, device_id=partner, device_id_type=MESH)
    pl.semaphore_wait(barrier, len(partners))

    started = []

    def send(src, dst, device):
        slot = len(started)
        copy = pltpu.make_async_remote_copy(
            src_ref=src,
            dst_ref=dst,
            send_sem=send_sem.at[slot],
            recv_sem=recv_sem.at[slot],
            device_id=device,
            device_id_type=MESH,
        )
        copy.start()
        started.append(copy)
        return copy

    f32 = jnp.float32
    bf16 = jnp.bfloat16

    def add_into(dst, count, reads):
        @pl.loop(0, count)
        def _(step):
            total = reads[0](step).astype(f32)
            for read in reads[1:]:
                total = total + read(step).astype(f32)
            dst(step, total.astype(bf16))

    core_copies = {}
    for d in (2, 1, 3, 0):
        j = (y + d) % 4
        core_copies[d] = send(term.at[1 - c, j], core_in.at[j], dev_core())

    def y_part(d, start, count, more=()):
        j = (y + d) % 4

        def put(step, value):
            y_sum[d, start + step // 4, step % 4] = value

        reads = [
            lambda step: term[c, j, start + step // 4, step % 4],
            lambda step: core_in[j, start + step // 4, step % 4],
        ]
        for slot in more:
            reads.append(lambda step, slot=slot: y_half[slot, step // 4, step % 4])
        add_into(put, 4 * count, reads)

    core_copies[2].wait_recv()
    y_part(2, 0, 2)
    half_0 = send(y_sum.at[2, pl.ds(0, 2)], y_half.at[0], dev_y(1))
    y_part(2, 2, 2)
    half_1 = send(y_sum.at[2, pl.ds(2, 2)], y_half.at[1], dev_y(3))
    core_copies[1].wait_recv()
    y_part(1, 2, 2)
    full_0b = send(y_sum.at[1, pl.ds(2, 2)], y_full.at[0, pl.ds(2, 2)], dev_y(1))
    core_copies[3].wait_recv()
    y_part(3, 0, 2)
    full_1a = send(y_sum.at[3, pl.ds(0, 2)], y_full.at[1, pl.ds(0, 2)], dev_y(3))
    half_0.wait_recv()
    y_part(1, 0, 2, more=(0,))
    full_0a = send(y_sum.at[1, pl.ds(0, 2)], y_full.at[0, pl.ds(0, 2)], dev_y(1))
    half_1.wait_recv()
    y_part(3, 2, 2, more=(1,))
    full_1b = send(y_sum.at[3, pl.ds(2, 2)], y_full.at[1, pl.ds(2, 2)], dev_y(3))
    core_copies[0].wait_recv()
    for copy in (full_0b, full_1a, full_0a, full_1b):
        copy.wait_recv()

    def x_part(d, start, count, more=()):
        q = (x + d) % 4

        def put(step, value):
            x_sum[d, start + step] = value

        reads = [
            lambda step: term[c, y, q, start + step],
            lambda step: core_in[y, q, start + step],
            lambda step: y_full[0, q, start + step],
            lambda step: y_full[1, q, start + step],
        ]
        for slot in more:
            reads.append(lambda step, slot=slot: x_half[slot, step])
        add_into(put, count, reads)

    x_part(2, 0, 2)
    half_0 = send(x_sum.at[2, pl.ds(0, 2)], x_half.at[0], dev_x(1))
    x_part(2, 2, 2)
    half_1 = send(x_sum.at[2, pl.ds(2, 2)], x_half.at[1], dev_x(3))
    x_part(1, 2, 2)
    full_0b = send(x_sum.at[1, pl.ds(2, 2)], x_full.at[0, pl.ds(2, 2)], dev_x(1))
    x_part(3, 0, 2)
    full_1a = send(x_sum.at[3, pl.ds(0, 2)], x_full.at[1, pl.ds(0, 2)], dev_x(3))
    half_0.wait_recv()
    x_part(1, 0, 2, more=(0,))
    full_0a = send(x_sum.at[1, pl.ds(0, 2)], x_full.at[0, pl.ds(0, 2)], dev_x(1))
    half_1.wait_recv()
    x_part(3, 2, 2, more=(1,))
    full_1b = send(x_sum.at[3, pl.ds(2, 2)], x_full.at[1, pl.ds(2, 2)], dev_x(3))
    x_part(0, 0, 4)
    for copy in (full_0b, full_1a, full_0a, full_1b):
        copy.wait_recv()

    z_copies = []
    for d in (3, 2, 1, 0):
        z = (zl + d) % 4
        z_sum[d] = (
            x_sum[0, z].astype(f32) + x_full[0, z].astype(f32) + x_full[1, z].astype(f32)
        ).astype(bf16)
        if d:
            z_copies.append(send(z_sum.at[d], z_in.at[d - 1], dev_z(d)))
    for copy in z_copies:
        copy.wait_recv()
    h_in[zh] = (
        (z_sum[0].astype(f32) + z_in[0].astype(f32))
        + (z_in[1].astype(f32) + z_in[2].astype(f32))
    ).astype(bf16)

    h_copies = [send(h_in.at[zh], h_in.at[zh], dev_h(d)) for d in (2, 1, 3)]
    for copy in h_copies:
        copy.wait_recv()
    grad[x] = (
        (h_in[0].astype(f32) + h_in[1].astype(f32)) + (h_in[2].astype(f32) + h_in[3].astype(f32))
    ).astype(bf16)

    left = (x + 3) % 4
    right = (x + 1) % 4
    to_right = send(grad.at[x], grad.at[x], dev_x(1))
    to_left = send(grad.at[x], grad.at[x], dev_x(3))
    to_right.wait_recv()
    on_right = send(grad.at[left, pl.ds(0, 4)], grad.at[left, pl.ds(0, 4)], dev_x(1))
    to_left.wait_recv()
    on_left = send(grad.at[right, pl.ds(4, 3)], grad.at[right, pl.ds(4, 3)], dev_x(3))
    on_right.wait_recv()
    on_left.wait_recv()

    decay = aux[0:1, :]
    decay_row = aux[0:1, 0:1]
    zero = jnp.zeros((1, 128), f32)
    zero_row = jnp.zeros((1, 1), f32)
    cols = [[zero, zero], [zero, zero]]
    mixed = [[zero, zero], [zero, zero]]
    rows = [zero_row, zero_row]
    for i in range(OWN):
        small = aux[8 + i : 9 + i, 0:128]
        is_kernel = (1.0 - small, small)
        for half in range(2):
            span = slice(16 * half, 16 * half + 16)
            squares = []
            for side in range(2):
                value = grad[2 * half + side, i].astype(f32)
                squares.append(value * value)
            mean = jnp.sum(squares[0] + squares[1], axis=1, keepdims=True) * (1.0 / CO)
            moment = decay_row * row_in[i, span, :] + (1.0 - decay_row) * mean
            new_row[i, span, :] = moment
            inverse = 1.0 / moment
            row_sum = jnp.sum(moment, axis=0, keepdims=True)
            for k in range(2):
                rows[k] = rows[k] + is_kernel[k][:, 0:1] * row_sum
            for side in range(2):
                plain = jnp.sum(squares[side], axis=0, keepdims=True)
                weighted = jnp.sum(squares[side] * inverse, axis=0, keepdims=True)
                for k in range(2):
                    cols[k][side] = cols[k][side] + is_kernel[k] * plain
                    mixed[k][side] = mixed[k][side] + is_kernel[k] * weighted
    for side in range(2):
        lanes = slice(128 * side, 128 * side + 128)
        for k in range(2):
            stat_own[k : k + 1, lanes] = cols[k][side]
            stat_own[2 + k : 3 + k, lanes] = mixed[k][side]
            stat_own[4 + k : 5 + k, lanes] = jnp.broadcast_to(rows[k], (1, 128))
        stat_own[6:8, lanes] = jnp.zeros((2, 128), f32)

    send(stat_own, stat_core, dev_core()).wait_recv()
    stat_y[y] = stat_own[...] + stat_core[...]
    y_copies = [send(stat_y.at[y], stat_y.at[y], dev_y(d)) for d in (2, 1, 3)]
    for copy in y_copies:
        copy.wait_recv()
    stat_z[zl] = (stat_y[0] + stat_y[1]) + (stat_y[2] + stat_y[3])
    z_copies = [send(stat_z.at[zl], stat_z.at[zl], dev_z(d)) for d in (3, 2, 1)]
    for copy in z_copies:
        copy.wait_recv()
    total = (stat_z[0] + stat_z[1]) + (stat_z[2] + stat_z[3])

    factors = []
    for k, rows_k in ((0, LARGE), (1, SMALL)):
        column = decay * aux[1 + k : 2 + k, :] + (1.0 - decay) * total[k : k + 1, :] / rows_k
        new_col[k : k + 1, :] = column
        row_mean = total[4 + k : 5 + k, 0:1] / rows_k
        square = row_mean * jnp.sum(total[2 + k : 3 + k, :] / column, axis=1, keepdims=True)
        clip = jnp.maximum(1.0, jnp.sqrt(square / (rows_k * CO)))
        factors.append(1.0 / (jnp.sqrt(column / row_mean) * clip))
    new_col[2:8, :] = jnp.zeros((6, 256), f32)

    for i in range(OWN):
        small = aux[8 + i : 9 + i, :]
        factor = (1.0 - small) * factors[0] + small * factors[1]
        for half in range(2):
            span = slice(16 * half, 16 * half + 16)
            scale = 1.0 / jnp.sqrt(new_row[i, span, :])
            for side in range(2):
                lanes = slice(128 * side, 128 * side + 128)
                value = grad[2 * half + side, i].astype(f32)
                change = value * scale * factor[:, lanes]
                update[i, span, lanes] = change
                fresh = master[i, span, lanes] - learn_rate * change
                new_master[i, span, lanes] = fresh
                quarter = 2 * half + side

                @pl.when(x == quarter)
                def _(fresh=fresh, quarter=quarter, i=i):
                    weights[c, y, quarter, zl, i] = fresh.astype(bf16)

    z_copies = [
        send(weights.at[c, y, x, zl], weights.at[c, y, x, zl], dev_z(d)) for d in (3, 2, 1)
    ]
    for copy in z_copies:
        copy.wait_recv()
    to_right = send(weights.at[c, y, x], weights.at[c, y, x], dev_x(1))
    to_left = send(weights.at[c, y, x], weights.at[c, y, x], dev_x(3))
    to_right.wait_recv()
    low, high = pl.ds(0, 2), pl.ds(2, 2)
    on_right = send(weights.at[c, y, left, low], weights.at[c, y, left, low], dev_x(1))
    to_left.wait_recv()
    on_left = send(weights.at[c, y, right, high], weights.at[c, y, right, high], dev_x(3))
    on_right.wait_recv()
    on_left.wait_recv()
    below = (y + 3) % 4
    above = (y + 1) % 4
    across = (y + 2) % 4
    to_above = send(weights.at[c, y], weights.at[c, y], dev_y(1))
    to_below = send(weights.at[c, y], weights.at[c, y], dev_y(3))
    cores = [send(weights.at[c, y], weights.at[c, y], dev_core())]
    to_above.wait_recv()
    on_above = send(weights.at[c, below, low], weights.at[c, below, low], dev_y(1))
    cores.append(send(weights.at[c, below], weights.at[c, below], dev_core()))
    to_below.wait_recv()
    on_below = send(weights.at[c, above, high], weights.at[c, above, high], dev_y(3))
    cores.append(send(weights.at[c, above], weights.at[c, above], dev_core()))
    on_above.wait_recv()
    cores.append(send(weights.at[c, across, low], weights.at[c, across, low], dev_core()))
    on_below.wait_recv()
    cores.append(send(weights.at[c, across, high], weights.at[c, across, high], dev_core()))
    for copy in cores:
        copy.wait_recv()
    assert len(started) == N_COPIES
    for copy in started:
        copy.wait_send()


N_COPIES = 49


def optimizer_step(term, aux, row_in, master):
    f32 = jnp.float32
    bf16 = jnp.bfloat16
    tile = (OWN, 16, 128)
    vmem = pl.BlockSpec(memory_space=pltpu.VMEM)
    return pl.pallas_call(
        step_kernel,
        name="optimizer_step",
        out_shape=(
            jax.ShapeDtypeStruct((OWN, 32, 256), f32),
            jax.ShapeDtypeStruct((OWN, 32, 256), f32),
            jax.ShapeDtypeStruct((OWN, 32, 1), f32),
            jax.ShapeDtypeStruct((8, 256), f32),
            jax.ShapeDtypeStruct((2, 4, 4, 4) + tile, bf16),
        ),
        in_specs=[vmem] * 4,
        out_specs=[vmem] * 5,
        scratch_shapes=[
            pltpu.VMEM((4, 4, 4) + tile, bf16),
            pltpu.VMEM((4, 4, 4) + tile, bf16),
            pltpu.VMEM((2, 2, 4) + tile, bf16),
            pltpu.VMEM((2, 4, 4) + tile, bf16),
            pltpu.VMEM((4, 4) + tile, bf16),
            pltpu.VMEM((2, 2) + tile, bf16),
            pltpu.VMEM((2, 4) + tile, bf16),
            pltpu.VMEM((4,) + tile, bf16),
            pltpu.VMEM((3,) + tile, bf16),
            pltpu.VMEM((4,) + tile, bf16),
            pltpu.VMEM((4,) + tile, bf16),
            pltpu.VMEM((8, 256), f32),
            pltpu.VMEM((8, 256), f32),
            pltpu.VMEM((4, 8, 256), f32),
            pltpu.VMEM((4, 8, 256), f32),
            pltpu.SemaphoreType.DMA((N_COPIES,)),
            pltpu.SemaphoreType.DMA((N_COPIES,)),
        ],
        compiler_params=pltpu.CompilerParams(collective_id=0, has_side_effects=True),
    )(term, aux, row_in, master)


def shift_columns(tiles, shifted):
    @pl.loop(0, (FR + 2) * (HW + 2))
    def _(step):
        frame, line = step // (HW + 2), step % (HW + 2)
        cells = tiles[0, frame, line].astype(jnp.float32)
        for off in range(3):
            shifted[off, frame, line] = cells[off : off + HW].astype(jnp.bfloat16)


def each_stored_block(order, visit):
    @pl.loop(0, 32)
    def _(owner):
        outer = (owner % 2) * 4 + (owner // 2) % 4
        for i in range(OWN):
            visit(order[owner * OWN + i], outer, (owner // 8) * OWN + i)


def backward_kernel(order, tiles, pre, grad_out, live, term, shifted, left, right, act, outer, inner):
    f32 = jnp.float32
    bf16 = jnp.bfloat16

    def note(block, outer_place, inner_place):
        outer[block] = outer_place
        inner[block] = inner_place

    each_stored_block(order, note)
    shift_columns(tiles, shifted)
    for part in range(4):
        rows = slice(128 * part, 128 * part + 128)
        values = pre[rows, :].astype(f32)
        sigma = jax.nn.sigmoid(values)
        act[rows, :] = (values * sigma).astype(bf16)
        cotangent = grad_out[rows, :]
        grad_act = lax.dot_general(
            cotangent, live[...], (((1,), (1,)), ((), ())), preferred_element_type=f32
        )
        grad_pre = grad_act * (sigma * (1.0 + values * (1.0 - sigma)))
        left[:, rows] = grad_pre.T.astype(bf16)
        right[:, rows] = cotangent.astype(f32).T.astype(bf16)

    def emit(first_block, product):
        result = product.T.astype(bf16)
        for j in range(8):
            block = first_block + j
            for q in range(4):
                row = 32 * j + 16 * (q // 2)
                lane = 128 * (q % 2)
                term[outer[block], q, inner[block]] = result[row : row + 16, lane : lane + 128]

    @pl.loop(0, 9)
    def _(spot):
        down, across = spot // 3, spot % 3
        for frame in range(3):
            window = shifted[across, frame : frame + FR, pl.ds(down, HW)].reshape(FR * HW * HW, CI)
            product = jnp.dot(left[...], window, preferred_element_type=f32)
            emit(8 * (9 * frame + spot), product)

    emit(NB3, jnp.dot(right[...], act[...], preferred_element_type=f32))


def backward(block_order, saved_tiles, pre_act, grad_output, pointwise_live):
    bf16 = jnp.bfloat16
    vmem = pl.BlockSpec(memory_space=pltpu.VMEM)
    smem = pl.BlockSpec(memory_space=pltpu.SMEM)
    return pl.pallas_call(
        backward_kernel,
        name="backward",
        out_shape=jax.ShapeDtypeStruct((8, 4, 28, 16, 128), bf16),
        in_specs=[smem] + [vmem] * 4,
        out_specs=vmem,
        scratch_shapes=[
            pltpu.VMEM((3, FR + 2, HW + 2, HW, CI), bf16),
            pltpu.VMEM((CO, FR * HW * HW), bf16),
            pltpu.VMEM((CO, FR * HW * HW), bf16),
            pltpu.VMEM((FR * HW * HW, CO), bf16),
            pltpu.SMEM((NB,), jnp.int32),
            pltpu.SMEM((NB,), jnp.int32),
        ],
    )(block_order, saved_tiles, pre_act, grad_output, pointwise_live)


def forward_kernel(
    order, tiles, gathered, update_in, master_in, output, update, master, shifted, kernels, hidden
):
    f32 = jnp.float32
    update[...] = update_in[...]
    master[...] = master_in[...]
    shift_columns(tiles, shifted)

    def place(block, outer, inner):
        for q in range(4):
            lane = 128 * (q % 2)
            kernels[block, q // 2, :, lane : lane + 128] = gathered[outer, q, inner]

    each_stored_block(order, place)
    hidden[...] = jnp.zeros_like(hidden)

    @pl.loop(0, 9)
    def _(spot):
        down, across = spot // 3, spot % 3
        for frame in range(3):
            window = shifted[across, frame : frame + FR, pl.ds(down, HW)].reshape(FR * HW * HW, CI)
            matrix = kernels[pl.ds(8 * (9 * frame + spot), 8)].reshape(CI, CO)
            hidden[...] += jnp.dot(window, matrix, preferred_element_type=f32)

    pointwise = kernels[NB3:NB].reshape(CO, CO)
    for part in range(4):
        rows = slice(128 * part, 128 * part + 128)
        values = hidden[rows, :]
        acted = (values * jax.nn.sigmoid(values)).astype(jnp.bfloat16)
        output[rows, :] = jnp.dot(acted, pointwise, preferred_element_type=f32).astype(jnp.bfloat16)


def forward(block_order, next_tiles, gathered, update, master):
    bf16 = jnp.bfloat16
    f32 = jnp.float32
    vmem = pl.BlockSpec(memory_space=pltpu.VMEM)
    smem = pl.BlockSpec(memory_space=pltpu.SMEM)
    return pl.pallas_call(
        forward_kernel,
        name="forward",
        out_shape=(
            jax.ShapeDtypeStruct((FR * HW * HW, CO), bf16),
            jax.ShapeDtypeStruct(update.shape, f32),
            jax.ShapeDtypeStruct(master.shape, f32),
        ),
        in_specs=[smem] + [vmem] * 4,
        out_specs=[vmem] * 3,
        scratch_shapes=[
            pltpu.VMEM((3, FR + 2, HW + 2, HW, CI), bf16),
            pltpu.VMEM((NB, 2, 16, CO), bf16),
            pltpu.VMEM((FR * HW * HW, CO), f32),
        ],
    )(block_order, next_tiles, gathered, update, master)


def shards(
    step_count,
    block_order,
    saved_tiles,
    pre_act,
    grad_output,
    pointwise_live,
    master_rows,
    row_moment,
    col_moment,
    next_tiles,
):
    term = backward(block_order, saved_tiles, pre_act, grad_output, pointwise_live)
    term = term.reshape(2, 4, 4, 4, OWN, 16, 128)
    owner = lax.axis_index("shard")
    own_blocks = lax.dynamic_slice_in_dim(block_order, owner * OWN, OWN)
    is_small = (own_blocks >= NB3).astype(jnp.float32)
    decay_rate = 1.0 - step_count.astype(jnp.float32)[0] ** (-decay_power)
    aux = jnp.concatenate(
        [
            jnp.broadcast_to(decay_rate, (1, CO)),
            col_moment,
            jnp.zeros((5, CO), jnp.float32),
            jnp.broadcast_to(is_small[:, None], (OWN, CO)),
            jnp.zeros((1, CO), jnp.float32),
        ],
        axis=0,
    )
    update, new_master, new_row, new_col, gathered = optimizer_step(
        term, aux, row_moment.reshape(OWN, BLK, 1), master_rows.reshape(OWN, BLK, CO)
    )
    next_output, update, new_master = forward(
        block_order, next_tiles, gathered.reshape(8, 4, 28, 16, 128), update, new_master
    )
    return (
        update.reshape(master_rows.shape),
        new_master.reshape(master_rows.shape),
        new_row.reshape(row_moment.shape),
        new_col[:2],
        next_output,
    )


def solution(mesh):
    in_specs = (
        P(),
        P(),
        P(("group", "shard"), None, None, None, None),
        P(("group", "shard"), None),
        P(("group", "shard"), None),
        P(),
        P("shard", None),
        P("shard"),
        P(),
        P(("group", "shard"), None, None, None, None),
    )
    out_specs = (P("shard", None), P("shard", None), P("shard"), P(), P(("group", "shard"), None))
    return jax.shard_map(shards, mesh=mesh, in_specs=in_specs, out_specs=out_specs, check_vma=False)
```

```python
import jax
import jax.numpy as jnp
from jax import lax
from jax.experimental import pallas as pl
from jax.experimental.pallas import tpu as pltpu
from jax.sharding import PartitionSpec as P

CI = 256
CO = 256
BLK = 32
FR = 2
HW = 16
NB3 = 216
NB = 224
OWN = 7
LARGE = 27.0 * CI
SMALL = 1.0 * CI

learn_rate = 0.002
decay_power = 0.8

MESH = pl.DeviceIdType.MESH


def step_kernel(
    term,
    aux,
    row_in,
    master,
    update,
    new_master,
    new_row,
    new_col,
    weights,
    core_in,
    first_sum,
    first_half,
    first_full,
    last_sum,
    last_half,
    last_full,
    z_sum,
    z_in,
    h_in,
    grad,
    stat_own,
    stat_core,
    stat_y,
    stat_z,
    send_sem,
    recv_sem,
):
    group = lax.axis_index("group")
    shard = lax.axis_index("shard")
    x = group // 4
    zh = group % 4
    c = shard % 2
    y = (shard // 2) % 4
    zl = shard // 8

    def dev_core():
        return (group, shard + 1 - 2 * c)

    def dev_y(d):
        return (group, zl * 8 + ((y + d) % 4) * 2 + c)

    def dev_z(d):
        return (group, ((zl + d) % 4) * 8 + y * 2 + c)

    def dev_x(d):
        return (((x + d) % 4) * 4 + zh, shard)

    def dev_h(d):
        return (x * 4 + (zh + d) % 4, shard)

    partners = [dev_core()]
    partners += [dev_y(d) for d in (1, 2, 3)]
    partners += [dev_x(d) for d in (1, 3)]
    partners += [dev_z(d) for d in (1, 2, 3)]
    partners += [dev_h(d) for d in (1, 2, 3)]
    barrier = pltpu.get_barrier_semaphore()
    for partner in partners:
        pl.semaphore_signal(barrier, inc=1, device_id=partner, device_id_type=MESH)
    pl.semaphore_wait(barrier, len(partners))

    started = []

    def send(src, dst, device):
        slot = len(started)
        copy = pltpu.make_async_remote_copy(
            src_ref=src,
            dst_ref=dst,
            send_sem=send_sem.at[slot],
            recv_sem=recv_sem.at[slot],
            device_id=device,
            device_id_type=MESH,
        )
        copy.start()
        started.append(copy)
        return copy

    f32 = jnp.float32
    bf16 = jnp.bfloat16

    def add_into(dst, count, reads):
        @pl.loop(0, count)
        def _(step):
            total = reads[0](step).astype(f32)
            for read in reads[1:]:
                total = total + read(step).astype(f32)
            dst(step, total.astype(bf16))

    coords = ((y, x), (x, y))
    devices = ((dev_y, dev_x), (dev_x, dev_y))

    def cell(stream, i, j):
        return (i, j) if stream == 0 else (j, i)

    core_copies = {}
    pair = (pl.ds(0, 2), pl.ds(2, 2))
    for d in (2, 1, 3, 0):
        j = (y + d) % 4
        core_copies[0, d] = send(
            term.at[1 - c, j, :, pair[0]], core_in.at[j, :, pair[0]], dev_core()
        )
        j = (x + d) % 4
        core_copies[1, d] = send(
            term.at[1 - c, :, j, pair[1]], core_in.at[:, j, pair[1]], dev_core()
        )

    def reduce_stream(stream):
        first, last = coords[stream]
        dev_first, dev_last = devices[stream]
        base = 2 * stream

        def first_part(d, start, more=()):
            i = (first + d) % 4

            def put(step, value):
                first_sum[stream, d, start + step // 2, step % 2] = value

            def here(step):
                return cell(stream, i, start + step // 2) + (base + step % 2,)

            reads = [
                lambda step: term[(c,) + here(step)],
                lambda step: core_in[here(step)],
            ]
            for slot in more:
                reads.append(lambda step, slot=slot: first_half[stream, slot, step // 2, step % 2])
            add_into(put, 4, reads)

        def pass_on(d, start, slot, step):
            span = pl.ds(start, 2)
            return send(
                first_sum.at[stream, d, span], first_full.at[stream, slot, span], dev_first(step)
            )

        core_copies[stream, 2].wait_recv()
        first_part(2, 0)
        half_0 = send(first_sum.at[stream, 2, pair[0]], first_half.at[stream, 0], dev_first(1))
        first_part(2, 2)
        half_1 = send(first_sum.at[stream, 2, pair[1]], first_half.at[stream, 1], dev_first(3))
        yield
        core_copies[stream, 1].wait_recv()
        first_part(1, 2)
        fulls = [pass_on(1, 2, 0, 1)]
        core_copies[stream, 3].wait_recv()
        first_part(3, 0)
        fulls.append(pass_on(3, 0, 1, 3))
        yield
        half_0.wait_recv()
        first_part(1, 0, more=(0,))
        fulls.append(pass_on(1, 0, 0, 1))
        half_1.wait_recv()
        first_part(3, 2, more=(1,))
        fulls.append(pass_on(3, 2, 1, 3))
        core_copies[stream, 0].wait_recv()
        yield
        for copy in fulls:
            copy.wait_recv()

        def last_part(d, start, count, more=()):
            q = (last + d) % 4
            place = cell(stream, first, q)

            def put(step, value):
                last_sum[stream, d, start + step] = value

            reads = [
                lambda step: term[(c,) + place + (base + start + step,)],
                lambda step: core_in[place + (base + start + step,)],
                lambda step: first_full[stream, 0, q, start + step],
                lambda step: first_full[stream, 1, q, start + step],
            ]
            for slot in more:
                reads.append(lambda step, slot=slot: last_half[stream, slot])
            add_into(put, count, reads)

        def pass_last(d, start, slot, step):
            return send(
                last_sum.at[stream, d, start], last_full.at[stream, slot, start], dev_last(step)
            )

        last_part(2, 0, 1)
        half_0 = send(last_sum.at[stream, 2, 0], last_half.at[stream, 0], dev_last(1))
        last_part(2, 1, 1)
        half_1 = send(last_sum.at[stream, 2, 1], last_half.at[stream, 1], dev_last(3))
        last_part(1, 1, 1)
        fulls = [pass_last(1, 1, 0, 1)]
        last_part(3, 0, 1)
        fulls.append(pass_last(3, 0, 1, 3))
        last_part(0, 0, 2)
        yield
        half_0.wait_recv()
        last_part(1, 0, 1, more=(0,))
        fulls.append(pass_last(1, 0, 0, 1))
        half_1.wait_recv()
        last_part(3, 1, 1, more=(1,))
        fulls.append(pass_last(3, 1, 1, 3))
        yield
        for copy in fulls:
            copy.wait_recv()
        yield

    for _ in zip(reduce_stream(0), reduce_stream(1)):
        pass

    z_copies = []
    for d in (3, 2, 1, 0):
        z = (zl + d) % 4
        z_sum[d] = (
            last_sum[z // 2, 0, z % 2].astype(f32)
            + last_full[z // 2, 0, z % 2].astype(f32)
            + last_full[z // 2, 1, z % 2].astype(f32)
        ).astype(bf16)
        if d:
            z_copies.append(send(z_sum.at[d], z_in.at[d - 1], dev_z(d)))
    for copy in z_copies:
        copy.wait_recv()
    h_in[zh] = (
        (z_sum[0].astype(f32) + z_in[0].astype(f32))
        + (z_in[1].astype(f32) + z_in[2].astype(f32))
    ).astype(bf16)

    h_copies = [send(h_in.at[zh], h_in.at[zh], dev_h(d)) for d in (2, 1, 3)]
    for copy in h_copies:
        copy.wait_recv()
    grad[x] = (
        (h_in[0].astype(f32) + h_in[1].astype(f32)) + (h_in[2].astype(f32) + h_in[3].astype(f32))
    ).astype(bf16)

    left = (x + 3) % 4
    right = (x + 1) % 4
    to_right = send(grad.at[x], grad.at[x], dev_x(1))
    to_left = send(grad.at[x], grad.at[x], dev_x(3))
    to_right.wait_recv()
    on_right = send(grad.at[left, pl.ds(0, 4)], grad.at[left, pl.ds(0, 4)], dev_x(1))
    to_left.wait_recv()
    on_left = send(grad.at[right, pl.ds(4, 3)], grad.at[right, pl.ds(4, 3)], dev_x(3))
    on_right.wait_recv()
    on_left.wait_recv()

    decay = aux[0:1, :]
    decay_row = aux[0:1, 0:1]
    zero = jnp.zeros((1, 128), f32)
    zero_row = jnp.zeros((1, 1), f32)
    cols = [[zero, zero], [zero, zero]]
    mixed = [[zero, zero], [zero, zero]]
    rows = [zero_row, zero_row]
    for i in range(OWN):
        small = aux[8 + i : 9 + i, 0:128]
        is_kernel = (1.0 - small, small)
        for half in range(2):
            span = slice(16 * half, 16 * half + 16)
            squares = []
            for side in range(2):
                value = grad[2 * half + side, i].astype(f32)
                squares.append(value * value)
            mean = jnp.sum(squares[0] + squares[1], axis=1, keepdims=True) * (1.0 / CO)
            moment = decay_row * row_in[i, span, :] + (1.0 - decay_row) * mean
            new_row[i, span, :] = moment
            inverse = 1.0 / moment
            row_sum = jnp.sum(moment, axis=0, keepdims=True)
            for k in range(2):
                rows[k] = rows[k] + is_kernel[k][:, 0:1] * row_sum
            for side in range(2):
                plain = jnp.sum(squares[side], axis=0, keepdims=True)
                weighted = jnp.sum(squares[side] * inverse, axis=0, keepdims=True)
                for k in range(2):
                    cols[k][side] = cols[k][side] + is_kernel[k] * plain
                    mixed[k][side] = mixed[k][side] + is_kernel[k] * weighted
    for side in range(2):
        lanes = slice(128 * side, 128 * side + 128)
        for k in range(2):
            stat_own[k : k + 1, lanes] = cols[k][side]
            stat_own[2 + k : 3 + k, lanes] = mixed[k][side]
            stat_own[4 + k : 5 + k, lanes] = jnp.broadcast_to(rows[k], (1, 128))
        stat_own[6:8, lanes] = jnp.zeros((2, 128), f32)

    send(stat_own, stat_core, dev_core()).wait_recv()
    stat_y[y] = stat_own[...] + stat_core[...]
    y_copies = [send(stat_y.at[y], stat_y.at[y], dev_y(d)) for d in (2, 1, 3)]
    for copy in y_copies:
        copy.wait_recv()
    stat_z[zl] = (stat_y[0] + stat_y[1]) + (stat_y[2] + stat_y[3])
    z_copies = [send(stat_z.at[zl], stat_z.at[zl], dev_z(d)) for d in (3, 2, 1)]
    for copy in z_copies:
        copy.wait_recv()
    total = (stat_z[0] + stat_z[1]) + (stat_z[2] + stat_z[3])

    factors = []
    for k, rows_k in ((0, LARGE), (1, SMALL)):
        column = decay * aux[1 + k : 2 + k, :] + (1.0 - decay) * total[k : k + 1, :] / rows_k
        new_col[k : k + 1, :] = column
        row_mean = total[4 + k : 5 + k, 0:1] / rows_k
        square = row_mean * jnp.sum(total[2 + k : 3 + k, :] / column, axis=1, keepdims=True)
        clip = jnp.maximum(1.0, jnp.sqrt(square / (rows_k * CO)))
        factors.append(1.0 / (jnp.sqrt(column / row_mean) * clip))
    new_col[2:8, :] = jnp.zeros((6, 256), f32)

    for i in range(OWN):
        small = aux[8 + i : 9 + i, :]
        factor = (1.0 - small) * factors[0] + small * factors[1]
        for half in range(2):
            span = slice(16 * half, 16 * half + 16)
            scale = 1.0 / jnp.sqrt(new_row[i, span, :])
            for side in range(2):
                lanes = slice(128 * side, 128 * side + 128)
                value = grad[2 * half + side, i].astype(f32)
                change = value * scale * factor[:, lanes]
                update[i, span, lanes] = change
                fresh = master[i, span, lanes] - learn_rate * change
                new_master[i, span, lanes] = fresh
                quarter = 2 * half + side

                @pl.when(x == quarter)
                def _(fresh=fresh, quarter=quarter, i=i):
                    weights[c, y, quarter, zl, i] = fresh.astype(bf16)

    z_copies = [
        send(weights.at[c, y, x, zl], weights.at[c, y, x, zl], dev_z(d)) for d in (3, 2, 1)
    ]
    for copy in z_copies:
        copy.wait_recv()
    cores = []

    def gather_stream(stream):
        first, last = coords[stream]
        dev_first, dev_last = devices[stream]
        base = 2 * stream
        both = pl.ds(base, 2)

        def spread(place, device):
            return send(weights.at[place], weights.at[place], device)

        def at_last(q, z):
            return (c,) + cell(stream, first, q) + (z,)

        def at_first(i, j):
            return (c,) + cell(stream, i, j) + (both,)

        up = spread(at_last(last, both), dev_last(1))
        down = spread(at_last(last, both), dev_last(3))
        up.wait_recv()
        on_up = spread(at_last((last + 3) % 4, base), dev_last(1))
        down.wait_recv()
        on_down = spread(at_last((last + 1) % 4, base + 1), dev_last(3))
        yield
        on_up.wait_recv()
        on_down.wait_recv()
        whole = slice(None)
        up = spread(at_first(first, whole), dev_first(1))
        down = spread(at_first(first, whole), dev_first(3))
        cores.append(spread(at_first(first, whole), dev_core()))
        yield
        before, after, across = (first + 3) % 4, (first + 1) % 4, (first + 2) % 4
        up.wait_recv()
        on_up = spread(at_first(before, pair[0]), dev_first(1))
        cores.append(spread(at_first(before, whole), dev_core()))
        down.wait_recv()
        on_down = spread(at_first(after, pair[1]), dev_first(3))
        cores.append(spread(at_first(after, whole), dev_core()))
        yield
        on_up.wait_recv()
        cores.append(spread(at_first(across, pair[0]), dev_core()))
        on_down.wait_recv()
        cores.append(spread(at_first(across, pair[1]), dev_core()))
        yield

    for _ in zip(gather_stream(0), gather_stream(1)):
        pass
    for copy in cores:
        copy.wait_recv()
    assert len(started) == N_COPIES
    for copy in started:
        copy.wait_send()


N_COPIES = 78


def optimizer_step(term, aux, row_in, master):
    f32 = jnp.float32
    bf16 = jnp.bfloat16
    tile = (OWN, 16, 128)
    vmem = pl.BlockSpec(memory_space=pltpu.VMEM)
    return pl.pallas_call(
        step_kernel,
        name="optimizer_step",
        out_shape=(
            jax.ShapeDtypeStruct((OWN, 32, 256), f32),
            jax.ShapeDtypeStruct((OWN, 32, 256), f32),
            jax.ShapeDtypeStruct((OWN, 32, 1), f32),
            jax.ShapeDtypeStruct((8, 256), f32),
            jax.ShapeDtypeStruct((2, 4, 4, 4) + tile, bf16),
        ),
        in_specs=[vmem] * 4,
        out_specs=[vmem] * 5,
        scratch_shapes=[
            pltpu.VMEM((4, 4, 4) + tile, bf16),
            pltpu.VMEM((2, 4, 4, 2) + tile, bf16),
            pltpu.VMEM((2, 2, 2, 2) + tile, bf16),
            pltpu.VMEM((2, 2, 4, 2) + tile, bf16),
            pltpu.VMEM((2, 4, 2) + tile, bf16),
            pltpu.VMEM((2, 2) + tile, bf16),
            pltpu.VMEM((2, 2, 2) + tile, bf16),
            pltpu.VMEM((4,) + tile, bf16),
            pltpu.VMEM((3,) + tile, bf16),
            pltpu.VMEM((4,) + tile, bf16),
            pltpu.VMEM((4,) + tile, bf16),
            pltpu.VMEM((8, 256), f32),
            pltpu.VMEM((8, 256), f32),
            pltpu.VMEM((4, 8, 256), f32),
            pltpu.VMEM((4, 8, 256), f32),
            pltpu.SemaphoreType.DMA((N_COPIES,)),
            pltpu.SemaphoreType.DMA((N_COPIES,)),
        ],
        compiler_params=pltpu.CompilerParams(collective_id=0, has_side_effects=True),
    )(term, aux, row_in, master)


def shift_columns(tiles, shifted):
    @pl.loop(0, (FR + 2) * (HW + 2))
    def _(step):
        frame, line = step // (HW + 2), step % (HW + 2)
        cells = tiles[0, frame, line].astype(jnp.float32)
        for off in range(3):
            shifted[off, frame, line] = cells[off : off + HW].astype(jnp.bfloat16)


def each_stored_block(order, visit):
    @pl.loop(0, 32)
    def _(owner):
        outer = (owner % 2) * 4 + (owner // 2) % 4
        for i in range(OWN):
            visit(order[owner * OWN + i], outer, (owner // 8) * OWN + i)


def diagonal(shape):
    return lax.broadcasted_iota(jnp.int32, shape, 0) == lax.broadcasted_iota(jnp.int32, shape, 1)


def backward_kernel(
    order,
    step_count,
    tiles,
    pre,
    grad_out,
    live,
    col_moment,
    row_moment,
    term,
    aux,
    row_column,
    shifted,
    left,
    right,
    act,
    outer,
    inner,
):
    f32 = jnp.float32
    owner = lax.axis_index("shard")
    steps = jnp.full((1, CO), step_count[0], jnp.int32).astype(f32)
    aux[0:1, :] = 1.0 - jnp.exp(-decay_power * jnp.log(steps))
    aux[1:3, :] = col_moment[...]
    aux[3:8, :] = jnp.zeros((5, CO), f32)
    for i in range(OWN):
        flag = jnp.where(order[owner * OWN + i] >= NB3, 1.0, 0.0).astype(f32)
        aux[8 + i : 9 + i, :] = jnp.full((1, CO), flag, f32)
    aux[15:16, :] = jnp.zeros((1, CO), f32)
    rows = OWN * BLK
    row_column[...] = jnp.sum(
        jnp.where(diagonal((rows, rows)), row_moment[...], 0.0), axis=1, keepdims=True
    )
    bf16 = jnp.bfloat16

    def note(block, outer_place, inner_place):
        outer[block] = outer_place
        inner[block] = inner_place

    each_stored_block(order, note)
    shift_columns(tiles, shifted)
    for part in range(4):
        rows = slice(128 * part, 128 * part + 128)
        values = pre[rows, :].astype(f32)
        sigma = jax.nn.sigmoid(values)
        act[rows, :] = (values * sigma).astype(bf16)
        cotangent = grad_out[rows, :]
        grad_act = lax.dot_general(
            cotangent, live[...], (((1,), (1,)), ((), ())), preferred_element_type=f32
        )
        grad_pre = grad_act * (sigma * (1.0 + values * (1.0 - sigma)))
        left[:, rows] = grad_pre.T.astype(bf16)
        right[:, rows] = cotangent.astype(f32).T.astype(bf16)

    def emit(first_block, product):
        result = product.T.astype(bf16)
        for j in range(8):
            block = first_block + j
            for q in range(4):
                row = 32 * j + 16 * (q // 2)
                lane = 128 * (q % 2)
                term[outer[block], q, inner[block]] = result[row : row + 16, lane : lane + 128]

    @pl.loop(0, 9)
    def _(spot):
        down, across = spot // 3, spot % 3
        for frame in range(3):
            window = shifted[across, frame : frame + FR, pl.ds(down, HW)].reshape(FR * HW * HW, CI)
            product = jnp.dot(left[...], window, preferred_element_type=f32)
            emit(8 * (9 * frame + spot), product)

    emit(NB3, jnp.dot(right[...], act[...], preferred_element_type=f32))


def backward(
    block_order,
    step_count,
    saved_tiles,
    pre_act,
    grad_output,
    pointwise_live,
    col_moment,
    row_moment,
):
    bf16 = jnp.bfloat16
    vmem = pl.BlockSpec(memory_space=pltpu.VMEM)
    smem = pl.BlockSpec(memory_space=pltpu.SMEM)
    return pl.pallas_call(
        backward_kernel,
        name="backward",
        out_shape=(
            jax.ShapeDtypeStruct((8, 4, 28, 16, 128), bf16),
            jax.ShapeDtypeStruct((16, CO), jnp.float32),
            jax.ShapeDtypeStruct((OWN * BLK, 1), jnp.float32),
        ),
        in_specs=[smem] * 2 + [vmem] * 6,
        out_specs=[vmem] * 3,
        scratch_shapes=[
            pltpu.VMEM((3, FR + 2, HW + 2, HW, CI), bf16),
            pltpu.VMEM((CO, FR * HW * HW), bf16),
            pltpu.VMEM((CO, FR * HW * HW), bf16),
            pltpu.VMEM((FR * HW * HW, CO), bf16),
            pltpu.SMEM((NB,), jnp.int32),
            pltpu.SMEM((NB,), jnp.int32),
        ],
    )(
        block_order,
        step_count,
        saved_tiles,
        pre_act,
        grad_output,
        pointwise_live,
        col_moment,
        row_moment.reshape(1, OWN * BLK),
    )


def forward_kernel(
    order,
    tiles,
    gathered,
    update_in,
    master_in,
    row_in,
    col_in,
    output,
    update,
    master,
    new_row,
    new_col,
    shifted,
    kernels,
    hidden,
):
    f32 = jnp.float32
    rows = OWN * BLK
    new_row[...] = jnp.sum(
        jnp.where(diagonal((rows, rows)), row_in[...], 0.0), axis=0, keepdims=True
    )
    new_col[...] = col_in[0:2, :]
    update[...] = update_in[...]
    master[...] = master_in[...]
    shift_columns(tiles, shifted)

    def place(block, outer, inner):
        for q in range(4):
            lane = 128 * (q % 2)
            kernels[block, q // 2, :, lane : lane + 128] = gathered[outer, q, inner]

    each_stored_block(order, place)
    hidden[...] = jnp.zeros_like(hidden)

    @pl.loop(0, 9)
    def _(spot):
        down, across = spot // 3, spot % 3
        for frame in range(3):
            window = shifted[across, frame : frame + FR, pl.ds(down, HW)].reshape(FR * HW * HW, CI)
            matrix = kernels[pl.ds(8 * (9 * frame + spot), 8)].reshape(CI, CO)
            hidden[...] += jnp.dot(window, matrix, preferred_element_type=f32)

    pointwise = kernels[NB3:NB].reshape(CO, CO)
    for part in range(4):
        rows = slice(128 * part, 128 * part + 128)
        values = hidden[rows, :]
        acted = (values * jax.nn.sigmoid(values)).astype(jnp.bfloat16)
        output[rows, :] = jnp.dot(acted, pointwise, preferred_element_type=f32).astype(jnp.bfloat16)


def forward(block_order, next_tiles, gathered, update, master, row, col):
    bf16 = jnp.bfloat16
    f32 = jnp.float32
    vmem = pl.BlockSpec(memory_space=pltpu.VMEM)
    smem = pl.BlockSpec(memory_space=pltpu.SMEM)
    return pl.pallas_call(
        forward_kernel,
        name="forward",
        out_shape=(
            jax.ShapeDtypeStruct((FR * HW * HW, CO), bf16),
            jax.ShapeDtypeStruct(update.shape, f32),
            jax.ShapeDtypeStruct(master.shape, f32),
            jax.ShapeDtypeStruct((1, OWN * BLK), f32),
            jax.ShapeDtypeStruct((2, CO), f32),
        ),
        in_specs=[smem] + [vmem] * 6,
        out_specs=[vmem] * 5,
        scratch_shapes=[
            pltpu.VMEM((3, FR + 2, HW + 2, HW, CI), bf16),
            pltpu.VMEM((NB, 2, 16, CO), bf16),
            pltpu.VMEM((FR * HW * HW, CO), f32),
        ],
    )(block_order, next_tiles, gathered, update, master, row, col)


def shards(
    step_count,
    block_order,
    saved_tiles,
    pre_act,
    grad_output,
    pointwise_live,
    master_rows,
    row_moment,
    col_moment,
    next_tiles,
):
    term, aux, row_column = backward(
        block_order,
        step_count,
        saved_tiles,
        pre_act,
        grad_output,
        pointwise_live,
        col_moment,
        row_moment,
    )
    term = term.reshape(2, 4, 4, 4, OWN, 16, 128)
    update, new_master, new_row, new_col, gathered = optimizer_step(
        term, aux, row_column.reshape(OWN, BLK, 1), master_rows.reshape(OWN, BLK, CO)
    )
    next_output, update, new_master, new_row, new_col = forward(
        block_order,
        next_tiles,
        gathered.reshape(8, 4, 28, 16, 128),
        update,
        new_master,
        new_row.reshape(OWN * BLK, 1),
        new_col,
    )
    return (
        update.reshape(master_rows.shape),
        new_master.reshape(master_rows.shape),
        new_row.reshape(row_moment.shape),
        new_col,
        next_output,
    )


def solution(mesh):
    in_specs = (
        P(),
        P(),
        P(("group", "shard"), None, None, None, None),
        P(("group", "shard"), None),
        P(("group", "shard"), None),
        P(),
        P("shard", None),
        P("shard"),
        P(),
        P(("group", "shard"), None, None, None, None),
    )
    out_specs = (P("shard", None), P("shard", None), P("shard"), P(), P(("group", "shard"), None))
    return jax.shard_map(shards, mesh=mesh, in_specs=in_specs, out_specs=out_specs, check_vma=False)
```

```python
import jax
import jax.numpy as jnp
from jax import lax
from jax.experimental import pallas as pl
from jax.experimental.pallas import tpu as pltpu
from jax.sharding import PartitionSpec as P

CI = 256
CO = 256
BLK = 32
FR = 2
HW = 16
NB3 = 216
NB = 224
OWN = 7
LARGE = 27.0 * CI
SMALL = 1.0 * CI

learn_rate = 0.002
decay_power = 0.8

MESH = pl.DeviceIdType.MESH


def step_kernel(
    term,
    aux,
    row_in,
    master,
    update,
    new_master,
    new_row,
    new_col,
    weights,
    core_in,
    first_sum,
    first_half,
    first_full,
    last_sum,
    last_half,
    last_full,
    z_sum,
    z_in,
    h_in,
    grad,
    stat_own,
    stat_core,
    stat_y,
    stat_z,
    send_sem,
    recv_sem,
):
    group = lax.axis_index("group")
    shard = lax.axis_index("shard")
    x = group // 4
    zh = group % 4
    c = shard % 2
    y = (shard // 2) % 4
    zl = shard // 8

    def dev_core():
        return (group, shard + 1 - 2 * c)

    def dev_y(d):
        return (group, zl * 8 + ((y + d) % 4) * 2 + c)

    def dev_z(d):
        return (group, ((zl + d) % 4) * 8 + y * 2 + c)

    def dev_x(d):
        return (((x + d) % 4) * 4 + zh, shard)

    def dev_h(d):
        return (x * 4 + (zh + d) % 4, shard)

    partners = [dev_core()]
    partners += [dev_y(d) for d in (1, 2, 3)]
    partners += [dev_x(d) for d in (1, 3)]
    partners += [dev_z(d) for d in (1, 2, 3)]
    partners += [dev_h(d) for d in (1, 2, 3)]
    barrier = pltpu.get_barrier_semaphore()
    for partner in partners:
        pl.semaphore_signal(barrier, inc=1, device_id=partner, device_id_type=MESH)
    pl.semaphore_wait(barrier, len(partners))

    started = []

    def send(src, dst, device):
        slot = len(started)
        copy = pltpu.make_async_remote_copy(
            src_ref=src,
            dst_ref=dst,
            send_sem=send_sem.at[slot],
            recv_sem=recv_sem.at[slot],
            device_id=device,
            device_id_type=MESH,
        )
        copy.start()
        started.append(copy)
        return copy

    f32 = jnp.float32
    bf16 = jnp.bfloat16

    def add_into(dst, count, reads):
        @pl.loop(0, count)
        def _(step):
            total = reads[0](step).astype(f32)
            for read in reads[1:]:
                total = total + read(step).astype(f32)
            dst(step, total.astype(bf16))

    coords = ((y, x), (x, y))
    devices = ((dev_y, dev_x), (dev_x, dev_y))

    def cell(stream, i, j):
        return (i, j) if stream == 0 else (j, i)

    core_copies = {}
    pair = (pl.ds(0, 2), pl.ds(2, 2))
    for d in (2, 1, 3, 0):
        j = (y + d) % 4
        core_copies[0, d] = send(
            term.at[1 - c, j, :, pair[0]], core_in.at[j, :, pair[0]], dev_core()
        )
        j = (x + d) % 4
        core_copies[1, d] = send(
            term.at[1 - c, :, j, pair[1]], core_in.at[:, j, pair[1]], dev_core()
        )

    def reduce_stream(stream):
        first, last = coords[stream]
        dev_first, dev_last = devices[stream]
        base = 2 * stream

        def first_part(d, start, more=()):
            i = (first + d) % 4

            def put(step, value):
                first_sum[stream, d, start + step // 2, step % 2] = value

            def here(step):
                return cell(stream, i, start + step // 2) + (base + step % 2,)

            reads = [
                lambda step: term[(c,) + here(step)],
                lambda step: core_in[here(step)],
            ]
            for slot in more:
                reads.append(lambda step, slot=slot: first_half[stream, slot, step // 2, step % 2])
            add_into(put, 4, reads)

        def pass_on(d, start, slot, step):
            span = pl.ds(start, 2)
            return send(
                first_sum.at[stream, d, span], first_full.at[stream, slot, span], dev_first(step)
            )

        core_copies[stream, 2].wait_recv()
        first_part(2, 0)
        half_0 = send(first_sum.at[stream, 2, pair[0]], first_half.at[stream, 0], dev_first(1))
        first_part(2, 2)
        half_1 = send(first_sum.at[stream, 2, pair[1]], first_half.at[stream, 1], dev_first(3))
        yield
        core_copies[stream, 1].wait_recv()
        first_part(1, 2)
        fulls = [pass_on(1, 2, 0, 1)]
        core_copies[stream, 3].wait_recv()
        first_part(3, 0)
        fulls.append(pass_on(3, 0, 1, 3))
        yield
        half_0.wait_recv()
        first_part(1, 0, more=(0,))
        fulls.append(pass_on(1, 0, 0, 1))
        half_1.wait_recv()
        first_part(3, 2, more=(1,))
        fulls.append(pass_on(3, 2, 1, 3))
        core_copies[stream, 0].wait_recv()
        yield
        for copy in fulls:
            copy.wait_recv()

        def last_part(d, start, count, more=()):
            q = (last + d) % 4
            place = cell(stream, first, q)

            def put(step, value):
                last_sum[stream, d, start + step] = value

            reads = [
                lambda step: term[(c,) + place + (base + start + step,)],
                lambda step: core_in[place + (base + start + step,)],
                lambda step: first_full[stream, 0, q, start + step],
                lambda step: first_full[stream, 1, q, start + step],
            ]
            for slot in more:
                reads.append(lambda step, slot=slot: last_half[stream, slot])
            add_into(put, count, reads)

        def pass_last(d, start, slot, step):
            return send(
                last_sum.at[stream, d, start], last_full.at[stream, slot, start], dev_last(step)
            )

        last_part(2, 0, 1)
        half_0 = send(last_sum.at[stream, 2, 0], last_half.at[stream, 0], dev_last(1))
        last_part(2, 1, 1)
        half_1 = send(last_sum.at[stream, 2, 1], last_half.at[stream, 1], dev_last(3))
        last_part(1, 1, 1)
        fulls = [pass_last(1, 1, 0, 1)]
        last_part(3, 0, 1)
        fulls.append(pass_last(3, 0, 1, 3))
        last_part(0, 0, 2)
        yield
        half_0.wait_recv()
        last_part(1, 0, 1, more=(0,))
        fulls.append(pass_last(1, 0, 0, 1))
        half_1.wait_recv()
        last_part(3, 1, 1, more=(1,))
        fulls.append(pass_last(3, 1, 1, 3))
        yield
        for copy in fulls:
            copy.wait_recv()
        yield

    for _ in zip(reduce_stream(0), reduce_stream(1)):
        pass

    z_copies = []
    for d in (3, 2, 1, 0):
        z = (zl + d) % 4
        z_sum[d] = (
            last_sum[z // 2, 0, z % 2].astype(f32)
            + last_full[z // 2, 0, z % 2].astype(f32)
            + last_full[z // 2, 1, z % 2].astype(f32)
        ).astype(bf16)
        if d:
            z_copies.append(send(z_sum.at[d], z_in.at[d - 1], dev_z(d)))
    for copy in z_copies:
        copy.wait_recv()
    h_in[zh] = (
        (z_sum[0].astype(f32) + z_in[0].astype(f32))
        + (z_in[1].astype(f32) + z_in[2].astype(f32))
    ).astype(bf16)

    h_copies = [send(h_in.at[zh], h_in.at[zh], dev_h(d)) for d in (2, 1, 3)]
    for copy in h_copies:
        copy.wait_recv()
    grad[x] = (
        (h_in[0].astype(f32) + h_in[1].astype(f32)) + (h_in[2].astype(f32) + h_in[3].astype(f32))
    ).astype(bf16)

    left = (x + 3) % 4
    right = (x + 1) % 4
    to_right = send(grad.at[x], grad.at[x], dev_x(1))
    to_left = send(grad.at[x], grad.at[x], dev_x(3))
    to_right.wait_recv()
    on_right = send(grad.at[left, pl.ds(0, 4)], grad.at[left, pl.ds(0, 4)], dev_x(1))
    to_left.wait_recv()
    on_left = send(grad.at[right, pl.ds(4, 3)], grad.at[right, pl.ds(4, 3)], dev_x(3))
    on_right.wait_recv()
    on_left.wait_recv()

    decay = aux[0:1, :]
    decay_row = aux[0:1, 0:1]
    zero = jnp.zeros((1, 128), f32)
    zero_row = jnp.zeros((1, 1), f32)
    cols = [[zero, zero], [zero, zero]]
    mixed = [[zero, zero], [zero, zero]]
    rows = [zero_row, zero_row]
    for i in range(OWN):
        small = aux[8 + i : 9 + i, 0:128]
        is_kernel = (1.0 - small, small)
        for half in range(2):
            span = slice(16 * half, 16 * half + 16)
            squares = []
            for side in range(2):
                value = grad[2 * half + side, i].astype(f32)
                squares.append(value * value)
            mean = jnp.sum(squares[0] + squares[1], axis=1, keepdims=True) * (1.0 / CO)
            moment = decay_row * row_in[i, span, :] + (1.0 - decay_row) * mean
            new_row[i, span, :] = moment
            inverse = 1.0 / moment
            row_sum = jnp.sum(moment, axis=0, keepdims=True)
            for k in range(2):
                rows[k] = rows[k] + is_kernel[k][:, 0:1] * row_sum
            for side in range(2):
                plain = jnp.sum(squares[side], axis=0, keepdims=True)
                weighted = jnp.sum(squares[side] * inverse, axis=0, keepdims=True)
                for k in range(2):
                    cols[k][side] = cols[k][side] + is_kernel[k] * plain
                    mixed[k][side] = mixed[k][side] + is_kernel[k] * weighted
    for side in range(2):
        lanes = slice(128 * side, 128 * side + 128)
        for k in range(2):
            stat_own[k : k + 1, lanes] = cols[k][side]
            stat_own[2 + k : 3 + k, lanes] = mixed[k][side]
            stat_own[4 + k : 5 + k, lanes] = jnp.broadcast_to(rows[k], (1, 128))
        stat_own[6:8, lanes] = jnp.zeros((2, 128), f32)

    send(stat_own, stat_core, dev_core()).wait_recv()
    stat_y[y] = stat_own[...] + stat_core[...]
    y_copies = [send(stat_y.at[y], stat_y.at[y], dev_y(d)) for d in (2, 1, 3)]
    for copy in y_copies:
        copy.wait_recv()
    stat_z[zl] = (stat_y[0] + stat_y[1]) + (stat_y[2] + stat_y[3])
    z_copies = [send(stat_z.at[zl], stat_z.at[zl], dev_z(d)) for d in (3, 2, 1)]
    for copy in z_copies:
        copy.wait_recv()
    total = (stat_z[0] + stat_z[1]) + (stat_z[2] + stat_z[3])

    factors = []
    for k, rows_k in ((0, LARGE), (1, SMALL)):
        column = decay * aux[1 + k : 2 + k, :] + (1.0 - decay) * total[k : k + 1, :] / rows_k
        new_col[k : k + 1, :] = column
        row_mean = total[4 + k : 5 + k, 0:1] / rows_k
        square = row_mean * jnp.sum(total[2 + k : 3 + k, :] / column, axis=1, keepdims=True)
        clip = jnp.maximum(1.0, jnp.sqrt(square / (rows_k * CO)))
        factors.append(1.0 / (jnp.sqrt(column / row_mean) * clip))
    new_col[2:8, :] = jnp.zeros((6, 256), f32)

    for i in range(OWN):
        small = aux[8 + i : 9 + i, :]
        factor = (1.0 - small) * factors[0] + small * factors[1]
        for half in range(2):
            span = slice(16 * half, 16 * half + 16)
            scale = 1.0 / jnp.sqrt(new_row[i, span, :])
            for side in range(2):
                lanes = slice(128 * side, 128 * side + 128)
                value = grad[2 * half + side, i].astype(f32)
                change = value * scale * factor[:, lanes]
                update[i, span, lanes] = change
                fresh = master[i, span, lanes] - learn_rate * change
                new_master[i, span, lanes] = fresh
                quarter = 2 * half + side

                @pl.when(x == quarter)
                def _(fresh=fresh, quarter=quarter, i=i):
                    weights[c, y, quarter, zl, i] = fresh.astype(bf16)

    z_copies = [
        send(weights.at[c, y, x, zl], weights.at[c, y, x, zl], dev_z(d)) for d in (3, 2, 1)
    ]
    for copy in z_copies:
        copy.wait_recv()
    cores = []

    def gather_stream(stream):
        first, last = coords[stream]
        dev_first, dev_last = devices[stream]
        base = 2 * stream
        both = pl.ds(base, 2)

        def spread(place, device):
            return send(weights.at[place], weights.at[place], device)

        def at_last(q, z):
            return (c,) + cell(stream, first, q) + (z,)

        def at_first(i, j):
            return (c,) + cell(stream, i, j) + (both,)

        up = spread(at_last(last, both), dev_last(1))
        down = spread(at_last(last, both), dev_last(3))
        up.wait_recv()
        on_up = spread(at_last((last + 3) % 4, base), dev_last(1))
        down.wait_recv()
        on_down = spread(at_last((last + 1) % 4, base + 1), dev_last(3))
        yield
        on_up.wait_recv()
        on_down.wait_recv()
        whole = slice(None)
        up = spread(at_first(first, whole), dev_first(1))
        down = spread(at_first(first, whole), dev_first(3))
        cores.append(spread(at_first(first, whole), dev_core()))
        yield
        before, after, across = (first + 3) % 4, (first + 1) % 4, (first + 2) % 4
        up.wait_recv()
        on_up = spread(at_first(before, pair[0]), dev_first(1))
        cores.append(spread(at_first(before, whole), dev_core()))
        down.wait_recv()
        on_down = spread(at_first(after, pair[1]), dev_first(3))
        cores.append(spread(at_first(after, whole), dev_core()))
        yield
        on_up.wait_recv()
        cores.append(spread(at_first(across, pair[0]), dev_core()))
        on_down.wait_recv()
        cores.append(spread(at_first(across, pair[1]), dev_core()))
        yield

    for _ in zip(gather_stream(0), gather_stream(1)):
        pass
    for copy in cores:
        copy.wait_recv()
    assert len(started) == N_COPIES
    for copy in started:
        copy.wait_send()


N_COPIES = 78
VMEM_GRANT = 28 * 1024 * 1024


def optimizer_step(term, aux, row_in, master):
    f32 = jnp.float32
    bf16 = jnp.bfloat16
    tile = (OWN, 16, 128)
    vmem = pl.BlockSpec(memory_space=pltpu.VMEM)
    return pl.pallas_call(
        step_kernel,
        name="optimizer_step",
        out_shape=(
            jax.ShapeDtypeStruct((OWN, 32, 256), f32),
            jax.ShapeDtypeStruct((OWN, 32, 256), f32),
            jax.ShapeDtypeStruct((OWN, 32, 1), f32),
            jax.ShapeDtypeStruct((8, 256), f32),
            jax.ShapeDtypeStruct((2, 4, 4, 4) + tile, bf16),
        ),
        in_specs=[vmem] * 4,
        out_specs=[vmem] * 5,
        scratch_shapes=[
            pltpu.VMEM((4, 4, 4) + tile, bf16),
            pltpu.VMEM((2, 4, 4, 2) + tile, bf16),
            pltpu.VMEM((2, 2, 2, 2) + tile, bf16),
            pltpu.VMEM((2, 2, 4, 2) + tile, bf16),
            pltpu.VMEM((2, 4, 2) + tile, bf16),
            pltpu.VMEM((2, 2) + tile, bf16),
            pltpu.VMEM((2, 2, 2) + tile, bf16),
            pltpu.VMEM((4,) + tile, bf16),
            pltpu.VMEM((3,) + tile, bf16),
            pltpu.VMEM((4,) + tile, bf16),
            pltpu.VMEM((4,) + tile, bf16),
            pltpu.VMEM((8, 256), f32),
            pltpu.VMEM((8, 256), f32),
            pltpu.VMEM((4, 8, 256), f32),
            pltpu.VMEM((4, 8, 256), f32),
            pltpu.SemaphoreType.DMA((N_COPIES,)),
            pltpu.SemaphoreType.DMA((N_COPIES,)),
        ],
        compiler_params=pltpu.CompilerParams(
            collective_id=0, has_side_effects=True, vmem_limit_bytes=VMEM_GRANT
        ),
    )(term, aux, row_in, master)


def shift_columns(tiles, shifted):
    @pl.loop(0, (FR + 2) * (HW + 2), unroll=9)
    def _(step):
        frame, line = step // (HW + 2), step % (HW + 2)
        cells = tiles[0, frame, line].astype(jnp.float32)
        for off in range(3):
            shifted[off, frame, line] = cells[off : off + HW].astype(jnp.bfloat16)


def each_stored_block(order, visit):
    @pl.loop(0, 32, unroll=4)
    def _(owner):
        outer = (owner % 2) * 4 + (owner // 2) % 4
        for i in range(OWN):
            visit(order[owner * OWN + i], outer, (owner // 8) * OWN + i)


def diagonal(shape):
    return lax.broadcasted_iota(jnp.int32, shape, 0) == lax.broadcasted_iota(jnp.int32, shape, 1)


def backward_kernel(
    order,
    step_count,
    tiles,
    pre,
    grad_out,
    live,
    col_moment,
    row_moment,
    term,
    aux,
    row_column,
    shifted,
    left,
    right,
    act,
    outer,
    inner,
):
    f32 = jnp.float32
    owner = lax.axis_index("shard")
    steps = jnp.full((1, CO), step_count[0], jnp.int32).astype(f32)
    aux[0:1, :] = 1.0 - jnp.exp(-decay_power * jnp.log(steps))
    aux[1:3, :] = col_moment[...]
    aux[3:8, :] = jnp.zeros((5, CO), f32)
    for i in range(OWN):
        flag = jnp.where(order[owner * OWN + i] >= NB3, 1.0, 0.0).astype(f32)
        aux[8 + i : 9 + i, :] = jnp.full((1, CO), flag, f32)
    aux[15:16, :] = jnp.zeros((1, CO), f32)
    rows = OWN * BLK
    row_column[...] = jnp.sum(
        jnp.where(diagonal((rows, rows)), row_moment[...], 0.0), axis=1, keepdims=True
    )
    bf16 = jnp.bfloat16

    def note(block, outer_place, inner_place):
        outer[block] = outer_place
        inner[block] = inner_place

    each_stored_block(order, note)
    shift_columns(tiles, shifted)
    for part in range(4):
        rows = slice(128 * part, 128 * part + 128)
        values = pre[rows, :].astype(f32)
        sigma = jax.nn.sigmoid(values)
        act[rows, :] = (values * sigma).astype(bf16)
        cotangent = grad_out[rows, :]
        grad_act = lax.dot_general(
            cotangent, live[...], (((1,), (1,)), ((), ())), preferred_element_type=f32
        )
        grad_pre = grad_act * (sigma * (1.0 + values * (1.0 - sigma)))
        left[:, rows] = grad_pre.T.astype(bf16)
        right[:, rows] = cotangent.astype(f32).T.astype(bf16)

    def emit(first_block, product):
        result = product.T.astype(bf16)
        for j in range(8):
            block = first_block + j
            for q in range(4):
                row = 32 * j + 16 * (q // 2)
                lane = 128 * (q % 2)
                term[outer[block], q, inner[block]] = result[row : row + 16, lane : lane + 128]

    @pl.loop(0, 9, unroll=3)
    def _(spot):
        down, across = spot // 3, spot % 3
        for frame in range(3):
            window = shifted[across, frame : frame + FR, pl.ds(down, HW)].reshape(FR * HW * HW, CI)
            product = jnp.dot(left[...], window, preferred_element_type=f32)
            emit(8 * (9 * frame + spot), product)

    emit(NB3, jnp.dot(right[...], act[...], preferred_element_type=f32))


def backward(
    block_order,
    step_count,
    saved_tiles,
    pre_act,
    grad_output,
    pointwise_live,
    col_moment,
    row_moment,
):
    bf16 = jnp.bfloat16
    vmem = pl.BlockSpec(memory_space=pltpu.VMEM)
    smem = pl.BlockSpec(memory_space=pltpu.SMEM)
    return pl.pallas_call(
        backward_kernel,
        name="backward",
        out_shape=(
            jax.ShapeDtypeStruct((8, 4, 28, 16, 128), bf16),
            jax.ShapeDtypeStruct((16, CO), jnp.float32),
            jax.ShapeDtypeStruct((OWN * BLK, 1), jnp.float32),
        ),
        in_specs=[smem] * 2 + [vmem] * 6,
        out_specs=[vmem] * 3,
        scratch_shapes=[
            pltpu.VMEM((3, FR + 2, HW + 2, HW, CI), bf16),
            pltpu.VMEM((CO, FR * HW * HW), bf16),
            pltpu.VMEM((CO, FR * HW * HW), bf16),
            pltpu.VMEM((FR * HW * HW, CO), bf16),
            pltpu.SMEM((NB,), jnp.int32),
            pltpu.SMEM((NB,), jnp.int32),
        ],
        compiler_params=pltpu.CompilerParams(vmem_limit_bytes=VMEM_GRANT),
    )(
        block_order,
        step_count,
        saved_tiles,
        pre_act,
        grad_output,
        pointwise_live,
        col_moment,
        row_moment.reshape(1, OWN * BLK),
    )


def forward_kernel(
    order,
    tiles,
    gathered,
    update_in,
    master_in,
    row_in,
    col_in,
    output,
    update,
    master,
    new_row,
    new_col,
    shifted,
    kernels,
    hidden,
):
    f32 = jnp.float32
    rows = OWN * BLK
    new_row[...] = jnp.sum(
        jnp.where(diagonal((rows, rows)), row_in[...], 0.0), axis=0, keepdims=True
    )
    new_col[...] = col_in[0:2, :]
    update[...] = update_in[...]
    master[...] = master_in[...]
    shift_columns(tiles, shifted)

    def place(block, outer, inner):
        for q in range(4):
            lane = 128 * (q % 2)
            kernels[block, q // 2, :, lane : lane + 128] = gathered[outer, q, inner]

    each_stored_block(order, place)
    hidden[...] = jnp.zeros_like(hidden)

    @pl.loop(0, 9, unroll=3)
    def _(spot):
        down, across = spot // 3, spot % 3
        for frame in range(3):
            window = shifted[across, frame : frame + FR, pl.ds(down, HW)].reshape(FR * HW * HW, CI)
            matrix = kernels[pl.ds(8 * (9 * frame + spot), 8)].reshape(CI, CO)
            hidden[...] += jnp.dot(window, matrix, preferred_element_type=f32)

    pointwise = kernels[NB3:NB].reshape(CO, CO)
    for part in range(4):
        rows = slice(128 * part, 128 * part + 128)
        values = hidden[rows, :]
        acted = (values * jax.nn.sigmoid(values)).astype(jnp.bfloat16)
        output[rows, :] = jnp.dot(acted, pointwise, preferred_element_type=f32).astype(jnp.bfloat16)


def forward(block_order, next_tiles, gathered, update, master, row, col):
    bf16 = jnp.bfloat16
    f32 = jnp.float32
    vmem = pl.BlockSpec(memory_space=pltpu.VMEM)
    smem = pl.BlockSpec(memory_space=pltpu.SMEM)
    return pl.pallas_call(
        forward_kernel,
        name="forward",
        out_shape=(
            jax.ShapeDtypeStruct((FR * HW * HW, CO), bf16),
            jax.ShapeDtypeStruct(update.shape, f32),
            jax.ShapeDtypeStruct(master.shape, f32),
            jax.ShapeDtypeStruct((1, OWN * BLK), f32),
            jax.ShapeDtypeStruct((2, CO), f32),
        ),
        in_specs=[smem] + [vmem] * 6,
        out_specs=[vmem] * 5,
        scratch_shapes=[
            pltpu.VMEM((3, FR + 2, HW + 2, HW, CI), bf16),
            pltpu.VMEM((NB, 2, 16, CO), bf16),
            pltpu.VMEM((FR * HW * HW, CO), f32),
        ],
        compiler_params=pltpu.CompilerParams(vmem_limit_bytes=VMEM_GRANT),
    )(block_order, next_tiles, gathered, update, master, row, col)


def shards(
    step_count,
    block_order,
    saved_tiles,
    pre_act,
    grad_output,
    pointwise_live,
    master_rows,
    row_moment,
    col_moment,
    next_tiles,
):
    term, aux, row_column = backward(
        block_order,
        step_count,
        saved_tiles,
        pre_act,
        grad_output,
        pointwise_live,
        col_moment,
        row_moment,
    )
    term = term.reshape(2, 4, 4, 4, OWN, 16, 128)
    update, new_master, new_row, new_col, gathered = optimizer_step(
        term, aux, row_column.reshape(OWN, BLK, 1), master_rows.reshape(OWN, BLK, CO)
    )
    next_output, update, new_master, new_row, new_col = forward(
        block_order,
        next_tiles,
        gathered.reshape(8, 4, 28, 16, 128),
        update,
        new_master,
        new_row.reshape(OWN * BLK, 1),
        new_col,
    )
    return (
        update.reshape(master_rows.shape),
        new_master.reshape(master_rows.shape),
        new_row.reshape(row_moment.shape),
        new_col,
        next_output,
    )


def solution(mesh):
    in_specs = (
        P(),
        P(),
        P(("group", "shard"), None, None, None, None),
        P(("group", "shard"), None),
        P(("group", "shard"), None),
        P(),
        P("shard", None),
        P("shard"),
        P(),
        P(("group", "shard"), None, None, None, None),
    )
    out_specs = (P("shard", None), P("shard", None), P("shard"), P(), P(("group", "shard"), None))
    return jax.shard_map(shards, mesh=mesh, in_specs=in_specs, out_specs=out_specs, check_vma=False)
```

```python
import jax
import jax.numpy as jnp
from jax import lax
from jax.experimental import pallas as pl
from jax.experimental.pallas import tpu as pltpu
from jax.sharding import PartitionSpec as P

CI = 256
CO = 256
BLK = 32
FR = 2
HW = 16
NB3 = 216
NB = 224
OWN = 7
LARGE = 27.0 * CI
SMALL = 1.0 * CI

learn_rate = 0.002
decay_power = 0.8

MESH = pl.DeviceIdType.MESH


def step_kernel(
    term,
    aux,
    row_in,
    master,
    update,
    new_master,
    new_row,
    new_col,
    weights,
    core_in,
    first_sum,
    first_half,
    first_full,
    last_sum,
    last_half,
    last_full,
    z_sum,
    z_in,
    h_in,
    grad,
    stat_own,
    stat_plane,
    stat_z,
    send_sem,
    recv_sem,
    relay,
):
    group = lax.axis_index("group")
    shard = lax.axis_index("shard")
    x = group // 4
    zh = group % 4
    c = shard % 2
    y = (shard // 2) % 4
    zl = shard // 8

    def dev_core():
        return (group, shard + 1 - 2 * c)

    def dev_y(d):
        return (group, zl * 8 + ((y + d) % 4) * 2 + c)

    def dev_z(d):
        return (group, ((zl + d) % 4) * 8 + y * 2 + c)

    def dev_x(d):
        return (((x + d) % 4) * 4 + zh, shard)

    def dev_plane(d, swap):
        core = c + swap * (1 - 2 * c)
        return (group, zl * 8 + ((y + d) % 4) * 2 + core)

    def dev_line(d):
        along = (zh * 4 + zl + d) % 16
        return (x * 4 + along // 4, (along % 4) * 8 + y * 2 + c)

    def dev_h(d):
        return (x * 4 + (zh + d) % 4, shard)

    partners = [dev_core()]
    partners += [dev_y(d) for d in (1, 2, 3)]
    partners += [dev_x(d) for d in (1, 3)]
    partners += [dev_z(d) for d in (1, 2, 3)]
    partners += [dev_line(d) for d in (1, 15)]
    partners += [dev_plane(d, 1) for d in (1, 2, 3)]
    barrier = pltpu.get_barrier_semaphore()
    for partner in partners:
        pl.semaphore_signal(barrier, inc=1, device_id=partner, device_id_type=MESH)
    pl.semaphore_wait(barrier, len(partners))

    def tell(slot, device):
        pl.semaphore_signal(relay.at[slot], inc=1, device_id=device, device_id_type=MESH)

    tell(0, dev_line(1))
    tell(1, dev_line(15))

    def relay_step(level):
        if level == 0:
            pl.semaphore_wait(relay.at[0], 1)
            pl.semaphore_wait(relay.at[1], 1)
            tell(2, dev_line(2))
            tell(3, dev_line(14))
        elif level == 2:
            pl.semaphore_wait(relay.at[2], 1)
            pl.semaphore_wait(relay.at[3], 1)
            tell(4, dev_line(4))
        elif level == 4:
            pl.semaphore_wait(relay.at[4], 1)

    started = []

    def send(src, dst, device):
        slot = len(started)
        copy = pltpu.make_async_remote_copy(
            src_ref=src,
            dst_ref=dst,
            send_sem=send_sem.at[slot],
            recv_sem=recv_sem.at[slot],
            device_id=device,
            device_id_type=MESH,
        )
        copy.start()
        started.append(copy)
        return copy

    f32 = jnp.float32
    bf16 = jnp.bfloat16

    def add_into(dst, count, reads):
        @pl.loop(0, count)
        def _(step):
            total = reads[0](step).astype(f32)
            for read in reads[1:]:
                total = total + read(step).astype(f32)
            dst(step, total.astype(bf16))

    coords = ((y, x), (x, y))
    devices = ((dev_y, dev_x), (dev_x, dev_y))

    def cell(stream, i, j):
        return (i, j) if stream == 0 else (j, i)

    core_copies = {}
    pair = (pl.ds(0, 2), pl.ds(2, 2))
    for d in (2, 1, 3, 0):
        j = (y + d) % 4
        core_copies[0, d] = send(
            term.at[1 - c, j, :, pair[0]], core_in.at[j, :, pair[0]], dev_core()
        )
        j = (x + d) % 4
        core_copies[1, d] = send(
            term.at[1 - c, :, j, pair[1]], core_in.at[:, j, pair[1]], dev_core()
        )

    def reduce_stream(stream):
        first, last = coords[stream]
        dev_first, dev_last = devices[stream]
        base = 2 * stream

        def first_part(d, start, more=()):
            i = (first + d) % 4

            def put(step, value):
                first_sum[stream, d, start + step // 2, step % 2] = value

            def here(step):
                return cell(stream, i, start + step // 2) + (base + step % 2,)

            reads = [
                lambda step: term[(c,) + here(step)],
                lambda step: core_in[here(step)],
            ]
            for slot in more:
                reads.append(lambda step, slot=slot: first_half[stream, slot, step // 2, step % 2])
            add_into(put, 4, reads)

        def pass_on(d, start, slot, step):
            span = pl.ds(start, 2)
            return send(
                first_sum.at[stream, d, span], first_full.at[stream, slot, span], dev_first(step)
            )

        core_copies[stream, 2].wait_recv()
        first_part(2, 0)
        half_0 = send(first_sum.at[stream, 2, pair[0]], first_half.at[stream, 0], dev_first(1))
        first_part(2, 2)
        half_1 = send(first_sum.at[stream, 2, pair[1]], first_half.at[stream, 1], dev_first(3))
        yield
        core_copies[stream, 1].wait_recv()
        first_part(1, 2)
        fulls = [pass_on(1, 2, 0, 1)]
        core_copies[stream, 3].wait_recv()
        first_part(3, 0)
        fulls.append(pass_on(3, 0, 1, 3))
        yield
        half_0.wait_recv()
        first_part(1, 0, more=(0,))
        fulls.append(pass_on(1, 0, 0, 1))
        half_1.wait_recv()
        first_part(3, 2, more=(1,))
        fulls.append(pass_on(3, 2, 1, 3))
        core_copies[stream, 0].wait_recv()
        yield
        for copy in fulls:
            copy.wait_recv()

        def last_part(d, start, count, more=()):
            q = (last + d) % 4
            place = cell(stream, first, q)

            def put(step, value):
                last_sum[stream, d, start + step] = value

            reads = [
                lambda step: term[(c,) + place + (base + start + step,)],
                lambda step: core_in[place + (base + start + step,)],
                lambda step: first_full[stream, 0, q, start + step],
                lambda step: first_full[stream, 1, q, start + step],
            ]
            for slot in more:
                reads.append(lambda step, slot=slot: last_half[stream, slot])
            add_into(put, count, reads)

        def pass_last(d, start, slot, step):
            return send(
                last_sum.at[stream, d, start], last_full.at[stream, slot, start], dev_last(step)
            )

        last_part(2, 0, 1)
        half_0 = send(last_sum.at[stream, 2, 0], last_half.at[stream, 0], dev_last(1))
        last_part(2, 1, 1)
        half_1 = send(last_sum.at[stream, 2, 1], last_half.at[stream, 1], dev_last(3))
        last_part(1, 1, 1)
        fulls = [pass_last(1, 1, 0, 1)]
        last_part(3, 0, 1)
        fulls.append(pass_last(3, 0, 1, 3))
        last_part(0, 0, 2)
        yield
        half_0.wait_recv()
        last_part(1, 0, 1, more=(0,))
        fulls.append(pass_last(1, 0, 0, 1))
        half_1.wait_recv()
        last_part(3, 1, 1, more=(1,))
        fulls.append(pass_last(3, 1, 1, 3))
        yield
        for copy in fulls:
            copy.wait_recv()
        yield

    for level, _ in enumerate(zip(reduce_stream(0), reduce_stream(1))):
        relay_step(level)

    z_copies = []
    for d in (3, 2, 1, 0):
        z = (zl + d) % 4
        z_sum[d] = (
            last_sum[z // 2, 0, z % 2].astype(f32)
            + last_full[z // 2, 0, z % 2].astype(f32)
            + last_full[z // 2, 1, z % 2].astype(f32)
        ).astype(bf16)
        if d:
            z_copies.append(send(z_sum.at[d], z_in.at[d - 1], dev_z(d)))
    for copy in z_copies:
        copy.wait_recv()
    h_in[zh] = (
        (z_sum[0].astype(f32) + z_in[0].astype(f32))
        + (z_in[1].astype(f32) + z_in[2].astype(f32))
    ).astype(bf16)

    h_copies = [send(h_in.at[zh], h_in.at[zh], dev_h(d)) for d in (2, 1, 3)]
    for copy in h_copies:
        copy.wait_recv()
    grad[x] = (
        (h_in[0].astype(f32) + h_in[1].astype(f32)) + (h_in[2].astype(f32) + h_in[3].astype(f32))
    ).astype(bf16)

    left = (x + 3) % 4
    right = (x + 1) % 4
    to_right = send(grad.at[x], grad.at[x], dev_x(1))
    to_left = send(grad.at[x], grad.at[x], dev_x(3))
    to_right.wait_recv()
    on_right = send(grad.at[left, pl.ds(0, 4)], grad.at[left, pl.ds(0, 4)], dev_x(1))
    to_left.wait_recv()
    on_left = send(grad.at[right, pl.ds(4, 3)], grad.at[right, pl.ds(4, 3)], dev_x(3))
    on_right.wait_recv()
    on_left.wait_recv()

    decay = aux[0:1, :]
    decay_row = aux[0:1, 0:1]
    zero = jnp.zeros((1, 128), f32)
    zero_row = jnp.zeros((1, 1), f32)
    cols = [[zero, zero], [zero, zero]]
    mixed = [[zero, zero], [zero, zero]]
    rows = [zero_row, zero_row]
    for i in range(OWN):
        small = aux[8 + i : 9 + i, 0:128]
        is_kernel = (1.0 - small, small)
        for half in range(2):
            span = slice(16 * half, 16 * half + 16)
            squares = []
            for side in range(2):
                value = grad[2 * half + side, i].astype(f32)
                squares.append(value * value)
            mean = jnp.sum(squares[0] + squares[1], axis=1, keepdims=True) * (1.0 / CO)
            moment = decay_row * row_in[i, span, :] + (1.0 - decay_row) * mean
            new_row[i, span, :] = moment
            inverse = 1.0 / moment
            row_sum = jnp.sum(moment, axis=0, keepdims=True)
            for k in range(2):
                rows[k] = rows[k] + is_kernel[k][:, 0:1] * row_sum
            for side in range(2):
                plain = jnp.sum(squares[side], axis=0, keepdims=True)
                weighted = jnp.sum(squares[side] * inverse, axis=0, keepdims=True)
                for k in range(2):
                    cols[k][side] = cols[k][side] + is_kernel[k] * plain
                    mixed[k][side] = mixed[k][side] + is_kernel[k] * weighted
    for side in range(2):
        lanes = slice(128 * side, 128 * side + 128)
        for k in range(2):
            stat_own[k : k + 1, lanes] = cols[k][side]
            stat_own[2 + k : 3 + k, lanes] = mixed[k][side]
            stat_own[4 + k : 5 + k, lanes] = jnp.broadcast_to(rows[k], (1, 128))
        stat_own[6:8, lanes] = jnp.zeros((2, 128), f32)

    stat_plane[c, y] = stat_own[...]
    plane_copies = [
        send(stat_plane.at[c, y], stat_plane.at[c, y], dev_plane(d, swap))
        for d, swap in ((2, 1), (2, 0), (1, 1), (3, 1), (1, 0), (3, 0), (0, 1))
    ]
    for copy in plane_copies:
        copy.wait_recv()
    by_core = [
        (stat_plane[k, 0] + stat_plane[k, 1]) + (stat_plane[k, 2] + stat_plane[k, 3])
        for k in range(2)
    ]
    stat_z[zl] = by_core[0] + by_core[1]
    z_copies = [send(stat_z.at[zl], stat_z.at[zl], dev_z(d)) for d in (3, 2, 1)]
    for copy in z_copies:
        copy.wait_recv()
    total = (stat_z[0] + stat_z[1]) + (stat_z[2] + stat_z[3])

    factors = []
    for k, rows_k in ((0, LARGE), (1, SMALL)):
        column = decay * aux[1 + k : 2 + k, :] + (1.0 - decay) * total[k : k + 1, :] / rows_k
        new_col[k : k + 1, :] = column
        row_mean = total[4 + k : 5 + k, 0:1] / rows_k
        square = row_mean * jnp.sum(total[2 + k : 3 + k, :] / column, axis=1, keepdims=True)
        clip = jnp.maximum(1.0, jnp.sqrt(square / (rows_k * CO)))
        factors.append(1.0 / (jnp.sqrt(column / row_mean) * clip))
    new_col[2:8, :] = jnp.zeros((6, 256), f32)

    for i in range(OWN):
        small = aux[8 + i : 9 + i, :]
        factor = (1.0 - small) * factors[0] + small * factors[1]
        for half in range(2):
            span = slice(16 * half, 16 * half + 16)
            scale = 1.0 / jnp.sqrt(new_row[i, span, :])
            for side in range(2):
                lanes = slice(128 * side, 128 * side + 128)
                value = grad[2 * half + side, i].astype(f32)
                change = value * scale * factor[:, lanes]
                update[i, span, lanes] = change
                fresh = master[i, span, lanes] - learn_rate * change
                new_master[i, span, lanes] = fresh
                quarter = 2 * half + side

                @pl.when(x == quarter)
                def _(fresh=fresh, quarter=quarter, i=i):
                    weights[c, y, quarter, zl, i] = fresh.astype(bf16)

    z_copies = [
        send(weights.at[c, y, x, zl], weights.at[c, y, x, zl], dev_z(d)) for d in (3, 2, 1)
    ]
    for copy in z_copies:
        copy.wait_recv()
    cores = []

    def gather_stream(stream):
        first, last = coords[stream]
        dev_first, dev_last = devices[stream]
        base = 2 * stream
        both = pl.ds(base, 2)

        def spread(place, device):
            return send(weights.at[place], weights.at[place], device)

        def at_last(q, z):
            return (c,) + cell(stream, first, q) + (z,)

        def at_first(i, j):
            return (c,) + cell(stream, i, j) + (both,)

        up = spread(at_last(last, both), dev_last(1))
        down = spread(at_last(last, both), dev_last(3))
        up.wait_recv()
        on_up = spread(at_last((last + 3) % 4, base), dev_last(1))
        down.wait_recv()
        on_down = spread(at_last((last + 1) % 4, base + 1), dev_last(3))
        yield
        on_up.wait_recv()
        on_down.wait_recv()
        whole = slice(None)
        up = spread(at_first(first, whole), dev_first(1))
        down = spread(at_first(first, whole), dev_first(3))
        cores.append(spread(at_first(first, whole), dev_core()))
        yield
        before, after, across = (first + 3) % 4, (first + 1) % 4, (first + 2) % 4
        up.wait_recv()
        on_up = spread(at_first(before, pair[0]), dev_first(1))
        cores.append(spread(at_first(before, whole), dev_core()))
        down.wait_recv()
        on_down = spread(at_first(after, pair[1]), dev_first(3))
        cores.append(spread(at_first(after, whole), dev_core()))
        yield
        on_up.wait_recv()
        cores.append(spread(at_first(across, pair[0]), dev_core()))
        on_down.wait_recv()
        cores.append(spread(at_first(across, pair[1]), dev_core()))
        yield

    for _ in zip(gather_stream(0), gather_stream(1)):
        pass
    for copy in cores:
        copy.wait_recv()
    assert len(started) == N_COPIES
    for copy in started:
        copy.wait_send()


N_COPIES = 81
VMEM_GRANT = 28 * 1024 * 1024


def optimizer_step(term, aux, row_in, master):
    f32 = jnp.float32
    bf16 = jnp.bfloat16
    tile = (OWN, 16, 128)
    vmem = pl.BlockSpec(memory_space=pltpu.VMEM)
    return pl.pallas_call(
        step_kernel,
        name="optimizer_step",
        out_shape=(
            jax.ShapeDtypeStruct((OWN, 32, 256), f32),
            jax.ShapeDtypeStruct((OWN, 32, 256), f32),
            jax.ShapeDtypeStruct((OWN, 32, 1), f32),
            jax.ShapeDtypeStruct((8, 256), f32),
            jax.ShapeDtypeStruct((2, 4, 4, 4) + tile, bf16),
        ),
        in_specs=[vmem] * 4,
        out_specs=[vmem] * 5,
        scratch_shapes=[
            pltpu.VMEM((4, 4, 4) + tile, bf16),
            pltpu.VMEM((2, 4, 4, 2) + tile, bf16),
            pltpu.VMEM((2, 2, 2, 2) + tile, bf16),
            pltpu.VMEM((2, 2, 4, 2) + tile, bf16),
            pltpu.VMEM((2, 4, 2) + tile, bf16),
            pltpu.VMEM((2, 2) + tile, bf16),
            pltpu.VMEM((2, 2, 2) + tile, bf16),
            pltpu.VMEM((4,) + tile, bf16),
            pltpu.VMEM((3,) + tile, bf16),
            pltpu.VMEM((4,) + tile, bf16),
            pltpu.VMEM((4,) + tile, bf16),
            pltpu.VMEM((8, 256), f32),
            pltpu.VMEM((2, 4, 8, 256), f32),
            pltpu.VMEM((4, 8, 256), f32),
            pltpu.SemaphoreType.DMA((N_COPIES,)),
            pltpu.SemaphoreType.DMA((N_COPIES,)),
            pltpu.SemaphoreType.REGULAR((5,)),
        ],
        compiler_params=pltpu.CompilerParams(
            collective_id=0, has_side_effects=True, vmem_limit_bytes=VMEM_GRANT
        ),
    )(term, aux, row_in, master)


def shift_columns(tiles, shifted):
    @pl.loop(0, (FR + 2) * (HW + 2), unroll=9)
    def _(step):
        frame, line = step // (HW + 2), step % (HW + 2)
        cells = tiles[0, frame, line].astype(jnp.float32)
        for off in range(3):
            shifted[off, frame, line] = cells[off : off + HW].astype(jnp.bfloat16)


def each_stored_block(order, visit):
    @pl.loop(0, 32, unroll=4)
    def _(owner):
        outer = (owner % 2) * 4 + (owner // 2) % 4
        for i in range(OWN):
            visit(order[owner * OWN + i], outer, (owner // 8) * OWN + i)


def diagonal(shape):
    return lax.broadcasted_iota(jnp.int32, shape, 0) == lax.broadcasted_iota(jnp.int32, shape, 1)


def backward_kernel(
    order,
    step_count,
    tiles,
    pre,
    grad_out,
    live,
    col_moment,
    row_moment,
    term,
    aux,
    row_column,
    shifted,
    left,
    right,
    act,
    outer,
    inner,
):
    f32 = jnp.float32
    owner = lax.axis_index("shard")
    steps = jnp.full((1, CO), step_count[0], jnp.int32).astype(f32)
    aux[0:1, :] = 1.0 - jnp.exp(-decay_power * jnp.log(steps))
    aux[1:3, :] = col_moment[...]
    aux[3:8, :] = jnp.zeros((5, CO), f32)
    for i in range(OWN):
        flag = jnp.where(order[owner * OWN + i] >= NB3, 1.0, 0.0).astype(f32)
        aux[8 + i : 9 + i, :] = jnp.full((1, CO), flag, f32)
    aux[15:16, :] = jnp.zeros((1, CO), f32)
    rows = OWN * BLK
    row_column[...] = jnp.sum(
        jnp.where(diagonal((rows, rows)), row_moment[...], 0.0), axis=1, keepdims=True
    )
    bf16 = jnp.bfloat16

    def note(block, outer_place, inner_place):
        outer[block] = outer_place
        inner[block] = inner_place

    each_stored_block(order, note)
    shift_columns(tiles, shifted)
    for part in range(4):
        rows = slice(128 * part, 128 * part + 128)
        values = pre[rows, :].astype(f32)
        sigma = jax.nn.sigmoid(values)
        act[rows, :] = (values * sigma).astype(bf16)
        cotangent = grad_out[rows, :]
        grad_act = lax.dot_general(
            cotangent, live[...], (((1,), (1,)), ((), ())), preferred_element_type=f32
        )
        grad_pre = grad_act * (sigma * (1.0 + values * (1.0 - sigma)))
        left[:, rows] = grad_pre.T.astype(bf16)
        right[:, rows] = cotangent.astype(f32).T.astype(bf16)

    def emit(first_block, product):
        result = product.T.astype(bf16)
        for j in range(8):
            block = first_block + j
            for q in range(4):
                row = 32 * j + 16 * (q // 2)
                lane = 128 * (q % 2)
                term[outer[block], q, inner[block]] = result[row : row + 16, lane : lane + 128]

    @pl.loop(0, 9, unroll=3)
    def _(spot):
        down, across = spot // 3, spot % 3
        for frame in range(3):
            window = shifted[across, frame : frame + FR, pl.ds(down, HW)].reshape(FR * HW * HW, CI)
            product = jnp.dot(left[...], window, preferred_element_type=f32)
            emit(8 * (9 * frame + spot), product)

    emit(NB3, jnp.dot(right[...], act[...], preferred_element_type=f32))


def backward(
    block_order,
    step_count,
    saved_tiles,
    pre_act,
    grad_output,
    pointwise_live,
    col_moment,
    row_moment,
):
    bf16 = jnp.bfloat16
    vmem = pl.BlockSpec(memory_space=pltpu.VMEM)
    smem = pl.BlockSpec(memory_space=pltpu.SMEM)
    return pl.pallas_call(
        backward_kernel,
        name="backward",
        out_shape=(
            jax.ShapeDtypeStruct((8, 4, 28, 16, 128), bf16),
            jax.ShapeDtypeStruct((16, CO), jnp.float32),
            jax.ShapeDtypeStruct((OWN * BLK, 1), jnp.float32),
        ),
        in_specs=[smem] * 2 + [vmem] * 6,
        out_specs=[vmem] * 3,
        scratch_shapes=[
            pltpu.VMEM((3, FR + 2, HW + 2, HW, CI), bf16),
            pltpu.VMEM((CO, FR * HW * HW), bf16),
            pltpu.VMEM((CO, FR * HW * HW), bf16),
            pltpu.VMEM((FR * HW * HW, CO), bf16),
            pltpu.SMEM((NB,), jnp.int32),
            pltpu.SMEM((NB,), jnp.int32),
        ],
        compiler_params=pltpu.CompilerParams(vmem_limit_bytes=VMEM_GRANT),
    )(
        block_order,
        step_count,
        saved_tiles,
        pre_act,
        grad_output,
        pointwise_live,
        col_moment,
        row_moment.reshape(1, OWN * BLK),
    )


def forward_kernel(
    order,
    tiles,
    gathered,
    update_in,
    master_in,
    row_in,
    col_in,
    output,
    update,
    master,
    new_row,
    new_col,
    shifted,
    kernels,
    hidden,
):
    f32 = jnp.float32
    rows = OWN * BLK
    new_row[...] = jnp.sum(
        jnp.where(diagonal((rows, rows)), row_in[...], 0.0), axis=0, keepdims=True
    )
    new_col[...] = col_in[0:2, :]
    update[...] = update_in[...]
    master[...] = master_in[...]
    shift_columns(tiles, shifted)

    def place(block, outer, inner):
        for q in range(4):
            lane = 128 * (q % 2)
            kernels[block, q // 2, :, lane : lane + 128] = gathered[outer, q, inner]

    each_stored_block(order, place)
    hidden[...] = jnp.zeros_like(hidden)

    @pl.loop(0, 9, unroll=3)
    def _(spot):
        down, across = spot // 3, spot % 3
        for frame in range(3):
            window = shifted[across, frame : frame + FR, pl.ds(down, HW)].reshape(FR * HW * HW, CI)
            matrix = kernels[pl.ds(8 * (9 * frame + spot), 8)].reshape(CI, CO)
            hidden[...] += jnp.dot(window, matrix, preferred_element_type=f32)

    pointwise = kernels[NB3:NB].reshape(CO, CO)
    for part in range(4):
        rows = slice(128 * part, 128 * part + 128)
        values = hidden[rows, :]
        acted = (values * jax.nn.sigmoid(values)).astype(jnp.bfloat16)
        output[rows, :] = jnp.dot(acted, pointwise, preferred_element_type=f32).astype(jnp.bfloat16)


def forward(block_order, next_tiles, gathered, update, master, row, col):
    bf16 = jnp.bfloat16
    f32 = jnp.float32
    vmem = pl.BlockSpec(memory_space=pltpu.VMEM)
    smem = pl.BlockSpec(memory_space=pltpu.SMEM)
    return pl.pallas_call(
        forward_kernel,
        name="forward",
        out_shape=(
            jax.ShapeDtypeStruct((FR * HW * HW, CO), bf16),
            jax.ShapeDtypeStruct(update.shape, f32),
            jax.ShapeDtypeStruct(master.shape, f32),
            jax.ShapeDtypeStruct((1, OWN * BLK), f32),
            jax.ShapeDtypeStruct((2, CO), f32),
        ),
        in_specs=[smem] + [vmem] * 6,
        out_specs=[vmem] * 5,
        scratch_shapes=[
            pltpu.VMEM((3, FR + 2, HW + 2, HW, CI), bf16),
            pltpu.VMEM((NB, 2, 16, CO), bf16),
            pltpu.VMEM((FR * HW * HW, CO), f32),
        ],
        compiler_params=pltpu.CompilerParams(vmem_limit_bytes=VMEM_GRANT),
    )(block_order, next_tiles, gathered, update, master, row, col)


def shards(
    step_count,
    block_order,
    saved_tiles,
    pre_act,
    grad_output,
    pointwise_live,
    master_rows,
    row_moment,
    col_moment,
    next_tiles,
):
    term, aux, row_column = backward(
        block_order,
        step_count,
        saved_tiles,
        pre_act,
        grad_output,
        pointwise_live,
        col_moment,
        row_moment,
    )
    term = term.reshape(2, 4, 4, 4, OWN, 16, 128)
    update, new_master, new_row, new_col, gathered = optimizer_step(
        term, aux, row_column.reshape(OWN, BLK, 1), master_rows.reshape(OWN, BLK, CO)
    )
    next_output, update, new_master, new_row, new_col = forward(
        block_order,
        next_tiles,
        gathered.reshape(8, 4, 28, 16, 128),
        update,
        new_master,
        new_row.reshape(OWN * BLK, 1),
        new_col,
    )
    return (
        update.reshape(master_rows.shape),
        new_master.reshape(master_rows.shape),
        new_row.reshape(row_moment.shape),
        new_col,
        next_output,
    )


def solution(mesh):
    in_specs = (
        P(),
        P(),
        P(("group", "shard"), None, None, None, None),
        P(("group", "shard"), None),
        P(("group", "shard"), None),
        P(),
        P("shard", None),
        P("shard"),
        P(),
        P(("group", "shard"), None, None, None, None),
    )
    out_specs = (P("shard", None), P("shard", None), P("shard"), P(), P(("group", "shard"), None))
    return jax.shard_map(shards, mesh=mesh, in_specs=in_specs, out_specs=out_specs, check_vma=False)
```

```python
import jax
import jax.numpy as jnp
from jax import lax
from jax.experimental import pallas as pl
from jax.experimental.pallas import tpu as pltpu
from jax.sharding import PartitionSpec as P

CI = 256
CO = 256
BLK = 32
FR = 2
HW = 16
NB3 = 216
NB = 224
OWN = 7
LARGE = 27.0 * CI
SMALL = 1.0 * CI

learn_rate = 0.002
decay_power = 0.8

MESH = pl.DeviceIdType.MESH


def step_kernel(
    term,
    aux,
    row_in,
    master,
    next_tiles,
    update,
    new_master,
    new_row,
    new_col,
    weights,
    next_shifted,
    core_in,
    first_sum,
    first_half,
    first_full,
    last_sum,
    last_half,
    last_full,
    z_sum,
    z_in,
    h_in,
    grad,
    stat_own,
    stat_plane,
    stat_z,
    send_sem,
    recv_sem,
    relay,
):
    group = lax.axis_index("group")
    shard = lax.axis_index("shard")
    x = group // 4
    zh = group % 4
    c = shard % 2
    y = (shard // 2) % 4
    zl = shard // 8

    def dev_core():
        return (group, shard + 1 - 2 * c)

    def dev_y(d):
        return (group, zl * 8 + ((y + d) % 4) * 2 + c)

    def dev_z(d):
        return (group, ((zl + d) % 4) * 8 + y * 2 + c)

    def dev_x(d):
        return (((x + d) % 4) * 4 + zh, shard)

    def dev_plane(d, swap):
        core = c + swap * (1 - 2 * c)
        return (group, zl * 8 + ((y + d) % 4) * 2 + core)

    def dev_line(d):
        along = (zh * 4 + zl + d) % 16
        return (x * 4 + along // 4, (along % 4) * 8 + y * 2 + c)

    def dev_h(d):
        return (x * 4 + (zh + d) % 4, shard)

    partners = [dev_core()]
    partners += [dev_y(d) for d in (1, 2, 3)]
    partners += [dev_x(d) for d in (1, 3)]
    partners += [dev_z(d) for d in (1, 2, 3)]
    partners += [dev_line(d) for d in (1, 15)]
    partners += [dev_plane(d, 1) for d in (1, 2, 3)]
    barrier = pltpu.get_barrier_semaphore()
    for partner in partners:
        pl.semaphore_signal(barrier, inc=1, device_id=partner, device_id_type=MESH)
    pl.semaphore_wait(barrier, len(partners))

    def tell(slot, device):
        pl.semaphore_signal(relay.at[slot], inc=1, device_id=device, device_id_type=MESH)

    tell(0, dev_line(1))
    tell(1, dev_line(15))

    def relay_step(level):
        if level == 0:
            pl.semaphore_wait(relay.at[0], 1)
            pl.semaphore_wait(relay.at[1], 1)
            tell(2, dev_line(2))
            tell(3, dev_line(14))
        elif level == 2:
            pl.semaphore_wait(relay.at[2], 1)
            pl.semaphore_wait(relay.at[3], 1)
            tell(4, dev_line(4))
        elif level == 4:
            pl.semaphore_wait(relay.at[4], 1)

    started = []

    def send(src, dst, device):
        slot = len(started)
        copy = pltpu.make_async_remote_copy(
            src_ref=src,
            dst_ref=dst,
            send_sem=send_sem.at[slot],
            recv_sem=recv_sem.at[slot],
            device_id=device,
            device_id_type=MESH,
        )
        copy.start()
        started.append(copy)
        return copy

    f32 = jnp.float32
    bf16 = jnp.bfloat16

    def add_into(dst, count, reads):
        @pl.loop(0, count, unroll=count)
        def _(step):
            total = reads[0](step).astype(f32)
            for read in reads[1:]:
                total = total + read(step).astype(f32)
            dst(step, total.astype(bf16))

    coords = ((y, x), (x, y))
    devices = ((dev_y, dev_x), (dev_x, dev_y))

    def cell(stream, i, j):
        return (i, j) if stream == 0 else (j, i)

    core_copies = {}
    pair = (pl.ds(0, 2), pl.ds(2, 2))
    for d in (2, 1, 3, 0):
        j = (y + d) % 4
        core_copies[0, d] = send(
            term.at[1 - c, j, :, pair[0]], core_in.at[j, :, pair[0]], dev_core()
        )
        j = (x + d) % 4
        core_copies[1, d] = send(
            term.at[1 - c, :, j, pair[1]], core_in.at[:, j, pair[1]], dev_core()
        )

    def reduce_stream(stream):
        first, last = coords[stream]
        dev_first, dev_last = devices[stream]
        base = 2 * stream

        def first_part(d, start, more=()):
            i = (first + d) % 4

            def put(step, value):
                first_sum[stream, d, start + step // 2, step % 2] = value

            def here(step):
                return cell(stream, i, start + step // 2) + (base + step % 2,)

            reads = [
                lambda step: term[(c,) + here(step)],
                lambda step: core_in[here(step)],
            ]
            for slot in more:
                reads.append(lambda step, slot=slot: first_half[stream, slot, step // 2, step % 2])
            add_into(put, 4, reads)

        def pass_on(d, start, slot, step):
            span = pl.ds(start, 2)
            return send(
                first_sum.at[stream, d, span], first_full.at[stream, slot, span], dev_first(step)
            )

        core_copies[stream, 2].wait_recv()
        first_part(2, 0)
        half_0 = send(first_sum.at[stream, 2, pair[0]], first_half.at[stream, 0], dev_first(1))
        first_part(2, 2)
        half_1 = send(first_sum.at[stream, 2, pair[1]], first_half.at[stream, 1], dev_first(3))
        yield
        core_copies[stream, 1].wait_recv()
        first_part(1, 2)
        fulls = [pass_on(1, 2, 0, 1)]
        core_copies[stream, 3].wait_recv()
        first_part(3, 0)
        fulls.append(pass_on(3, 0, 1, 3))
        yield
        half_0.wait_recv()
        first_part(1, 0, more=(0,))
        fulls.append(pass_on(1, 0, 0, 1))
        half_1.wait_recv()
        first_part(3, 2, more=(1,))
        fulls.append(pass_on(3, 2, 1, 3))
        core_copies[stream, 0].wait_recv()
        yield
        for copy in fulls:
            copy.wait_recv()

        def last_part(d, start, count, more=()):
            q = (last + d) % 4
            place = cell(stream, first, q)

            def put(step, value):
                last_sum[stream, d, start + step] = value

            reads = [
                lambda step: term[(c,) + place + (base + start + step,)],
                lambda step: core_in[place + (base + start + step,)],
                lambda step: first_full[stream, 0, q, start + step],
                lambda step: first_full[stream, 1, q, start + step],
            ]
            for slot in more:
                reads.append(lambda step, slot=slot: last_half[stream, slot])
            add_into(put, count, reads)

        def pass_last(d, start, slot, step):
            return send(
                last_sum.at[stream, d, start], last_full.at[stream, slot, start], dev_last(step)
            )

        last_part(2, 0, 1)
        half_0 = send(last_sum.at[stream, 2, 0], last_half.at[stream, 0], dev_last(1))
        last_part(2, 1, 1)
        half_1 = send(last_sum.at[stream, 2, 1], last_half.at[stream, 1], dev_last(3))
        last_part(1, 1, 1)
        fulls = [pass_last(1, 1, 0, 1)]
        last_part(3, 0, 1)
        fulls.append(pass_last(3, 0, 1, 3))
        last_part(0, 0, 2)
        yield
        half_0.wait_recv()
        last_part(1, 0, 1, more=(0,))
        fulls.append(pass_last(1, 0, 0, 1))
        half_1.wait_recv()
        last_part(3, 1, 1, more=(1,))
        fulls.append(pass_last(3, 1, 1, 3))
        yield
        for copy in fulls:
            copy.wait_recv()
        yield

    for level, _ in enumerate(zip(reduce_stream(0), reduce_stream(1))):
        relay_step(level)

    z_copies = []
    for d in (3, 2, 1, 0):
        z = (zl + d) % 4
        z_sum[d] = (
            last_sum[z // 2, 0, z % 2].astype(f32)
            + last_full[z // 2, 0, z % 2].astype(f32)
            + last_full[z // 2, 1, z % 2].astype(f32)
        ).astype(bf16)
        if d:
            z_copies.append(send(z_sum.at[d], z_in.at[d - 1], dev_z(d)))
    for copy in z_copies:
        copy.wait_recv()
    h_in[zh] = (
        (z_sum[0].astype(f32) + z_in[0].astype(f32))
        + (z_in[1].astype(f32) + z_in[2].astype(f32))
    ).astype(bf16)

    h_copies = [send(h_in.at[zh], h_in.at[zh], dev_h(d)) for d in (2, 1, 3)]
    shift_columns(next_tiles, next_shifted)
    for copy in h_copies:
        copy.wait_recv()
    grad[x] = (
        (h_in[0].astype(f32) + h_in[1].astype(f32)) + (h_in[2].astype(f32) + h_in[3].astype(f32))
    ).astype(bf16)

    left = (x + 3) % 4
    right = (x + 1) % 4
    to_right = send(grad.at[x], grad.at[x], dev_x(1))
    to_left = send(grad.at[x], grad.at[x], dev_x(3))
    to_right.wait_recv()
    on_right = send(grad.at[left, pl.ds(0, 4)], grad.at[left, pl.ds(0, 4)], dev_x(1))
    to_left.wait_recv()
    on_left = send(grad.at[right, pl.ds(4, 3)], grad.at[right, pl.ds(4, 3)], dev_x(3))
    on_right.wait_recv()
    on_left.wait_recv()

    decay = aux[0:1, :]
    decay_row = aux[0:1, 0:1]
    zero = jnp.zeros((1, 128), f32)
    zero_row = jnp.zeros((1, 1), f32)
    cols = [[zero, zero], [zero, zero]]
    mixed = [[zero, zero], [zero, zero]]
    rows = [zero_row, zero_row]
    for i in range(OWN):
        small = aux[8 + i : 9 + i, 0:128]
        is_kernel = (1.0 - small, small)
        for half in range(2):
            span = slice(16 * half, 16 * half + 16)
            squares = []
            for side in range(2):
                value = grad[2 * half + side, i].astype(f32)
                squares.append(value * value)
            mean = jnp.sum(squares[0] + squares[1], axis=1, keepdims=True) * (1.0 / CO)
            moment = decay_row * row_in[i, span, :] + (1.0 - decay_row) * mean
            new_row[i, span, :] = moment
            inverse = 1.0 / moment
            row_sum = jnp.sum(moment, axis=0, keepdims=True)
            for k in range(2):
                rows[k] = rows[k] + is_kernel[k][:, 0:1] * row_sum
            for side in range(2):
                plain = jnp.sum(squares[side], axis=0, keepdims=True)
                weighted = jnp.sum(squares[side] * inverse, axis=0, keepdims=True)
                for k in range(2):
                    cols[k][side] = cols[k][side] + is_kernel[k] * plain
                    mixed[k][side] = mixed[k][side] + is_kernel[k] * weighted
    for side in range(2):
        lanes = slice(128 * side, 128 * side + 128)
        for k in range(2):
            stat_own[k : k + 1, lanes] = cols[k][side]
            stat_own[2 + k : 3 + k, lanes] = mixed[k][side]
            stat_own[4 + k : 5 + k, lanes] = jnp.broadcast_to(rows[k], (1, 128))
        stat_own[6:8, lanes] = jnp.zeros((2, 128), f32)

    stat_plane[c, y] = stat_own[...]
    plane_copies = [
        send(stat_plane.at[c, y], stat_plane.at[c, y], dev_plane(d, swap))
        for d, swap in ((2, 1), (2, 0), (1, 1), (3, 1), (1, 0), (3, 0), (0, 1))
    ]
    for copy in plane_copies:
        copy.wait_recv()
    by_core = [
        (stat_plane[k, 0] + stat_plane[k, 1]) + (stat_plane[k, 2] + stat_plane[k, 3])
        for k in range(2)
    ]
    stat_z[zl] = by_core[0] + by_core[1]
    z_copies = [send(stat_z.at[zl], stat_z.at[zl], dev_z(d)) for d in (3, 2, 1)]
    for copy in z_copies:
        copy.wait_recv()
    total = (stat_z[0] + stat_z[1]) + (stat_z[2] + stat_z[3])

    factors = []
    for k, rows_k in ((0, LARGE), (1, SMALL)):
        column = decay * aux[1 + k : 2 + k, :] + (1.0 - decay) * total[k : k + 1, :] / rows_k
        new_col[k : k + 1, :] = column
        row_mean = total[4 + k : 5 + k, 0:1] / rows_k
        square = row_mean * jnp.sum(total[2 + k : 3 + k, :] / column, axis=1, keepdims=True)
        clip = jnp.maximum(1.0, jnp.sqrt(square / (rows_k * CO)))
        factors.append(1.0 / (jnp.sqrt(column / row_mean) * clip))
    new_col[2:8, :] = jnp.zeros((6, 256), f32)

    for i in range(OWN):
        small = aux[8 + i : 9 + i, :]
        factor = (1.0 - small) * factors[0] + small * factors[1]
        for half in range(2):
            span = slice(16 * half, 16 * half + 16)
            scale = 1.0 / jnp.sqrt(new_row[i, span, :])
            for side in range(2):
                lanes = slice(128 * side, 128 * side + 128)
                value = grad[2 * half + side, i].astype(f32)
                change = value * scale * factor[:, lanes]
                update[i, span, lanes] = change
                fresh = master[i, span, lanes] - learn_rate * change
                new_master[i, span, lanes] = fresh
                quarter = 2 * half + side

                @pl.when(x == quarter)
                def _(fresh=fresh, quarter=quarter, i=i):
                    weights[c, y, quarter, zl, i] = fresh.astype(bf16)

    z_copies = [
        send(weights.at[c, y, x, zl], weights.at[c, y, x, zl], dev_z(d)) for d in (3, 2, 1)
    ]
    for copy in z_copies:
        copy.wait_recv()
    cores = []

    def gather_stream(stream):
        first, last = coords[stream]
        dev_first, dev_last = devices[stream]
        base = 2 * stream
        both = pl.ds(base, 2)

        def spread(place, device):
            return send(weights.at[place], weights.at[place], device)

        def at_last(q, z):
            return (c,) + cell(stream, first, q) + (z,)

        def at_first(i, j):
            return (c,) + cell(stream, i, j) + (both,)

        up = spread(at_last(last, both), dev_last(1))
        down = spread(at_last(last, both), dev_last(3))
        up.wait_recv()
        on_up = spread(at_last((last + 3) % 4, base), dev_last(1))
        down.wait_recv()
        on_down = spread(at_last((last + 1) % 4, base + 1), dev_last(3))
        yield
        on_up.wait_recv()
        on_down.wait_recv()
        whole = slice(None)
        up = spread(at_first(first, whole), dev_first(1))
        down = spread(at_first(first, whole), dev_first(3))
        cores.append(spread(at_first(first, whole), dev_core()))
        yield
        before, after, across = (first + 3) % 4, (first + 1) % 4, (first + 2) % 4
        up.wait_recv()
        on_up = spread(at_first(before, pair[0]), dev_first(1))
        cores.append(spread(at_first(before, whole), dev_core()))
        down.wait_recv()
        on_down = spread(at_first(after, pair[1]), dev_first(3))
        cores.append(spread(at_first(after, whole), dev_core()))
        yield
        on_up.wait_recv()
        cores.append(spread(at_first(across, pair[0]), dev_core()))
        on_down.wait_recv()
        cores.append(spread(at_first(across, pair[1]), dev_core()))
        yield

    for _ in zip(gather_stream(0), gather_stream(1)):
        pass
    for copy in cores:
        copy.wait_recv()
    assert len(started) == N_COPIES
    for copy in started:
        copy.wait_send()


N_COPIES = 81
VMEM_GRANT = 28 * 1024 * 1024


def optimizer_step(term, aux, row_in, master, next_tiles):
    f32 = jnp.float32
    bf16 = jnp.bfloat16
    tile = (OWN, 16, 128)
    vmem = pl.BlockSpec(memory_space=pltpu.VMEM)
    return pl.pallas_call(
        step_kernel,
        name="optimizer_step",
        out_shape=(
            jax.ShapeDtypeStruct((OWN, 32, 256), f32),
            jax.ShapeDtypeStruct((OWN, 32, 256), f32),
            jax.ShapeDtypeStruct((OWN, 32, 1), f32),
            jax.ShapeDtypeStruct((8, 256), f32),
            jax.ShapeDtypeStruct((2, 4, 4, 4) + tile, bf16),
            jax.ShapeDtypeStruct((3, FR + 2, HW + 2, HW, CI), bf16),
        ),
        in_specs=[vmem] * 5,
        out_specs=[vmem] * 6,
        scratch_shapes=[
            pltpu.VMEM((4, 4, 4) + tile, bf16),
            pltpu.VMEM((2, 4, 4, 2) + tile, bf16),
            pltpu.VMEM((2, 2, 2, 2) + tile, bf16),
            pltpu.VMEM((2, 2, 4, 2) + tile, bf16),
            pltpu.VMEM((2, 4, 2) + tile, bf16),
            pltpu.VMEM((2, 2) + tile, bf16),
            pltpu.VMEM((2, 2, 2) + tile, bf16),
            pltpu.VMEM((4,) + tile, bf16),
            pltpu.VMEM((3,) + tile, bf16),
            pltpu.VMEM((4,) + tile, bf16),
            pltpu.VMEM((4,) + tile, bf16),
            pltpu.VMEM((8, 256), f32),
            pltpu.VMEM((2, 4, 8, 256), f32),
            pltpu.VMEM((4, 8, 256), f32),
            pltpu.SemaphoreType.DMA((N_COPIES,)),
            pltpu.SemaphoreType.DMA((N_COPIES,)),
            pltpu.SemaphoreType.REGULAR((5,)),
        ],
        compiler_params=pltpu.CompilerParams(
            collective_id=0, has_side_effects=True, vmem_limit_bytes=VMEM_GRANT
        ),
    )(term, aux, row_in, master, next_tiles)


def shift_columns(tiles, shifted):
    @pl.loop(0, (FR + 2) * (HW + 2), unroll=9)
    def _(step):
        frame, line = step // (HW + 2), step % (HW + 2)
        cells = tiles[0, frame, line].astype(jnp.float32)
        for off in range(3):
            shifted[off, frame, line] = cells[off : off + HW].astype(jnp.bfloat16)


def each_stored_block(order, visit):
    @pl.loop(0, 32, unroll=4)
    def _(owner):
        outer = (owner % 2) * 4 + (owner // 2) % 4
        for i in range(OWN):
            visit(order[owner * OWN + i], outer, (owner // 8) * OWN + i)


def diagonal(shape):
    return lax.broadcasted_iota(jnp.int32, shape, 0) == lax.broadcasted_iota(jnp.int32, shape, 1)


def backward_kernel(
    order,
    step_count,
    tiles,
    pre,
    grad_out,
    live,
    col_moment,
    row_moment,
    term,
    aux,
    row_column,
    shifted,
    left,
    right,
    act,
    outer,
    inner,
):
    f32 = jnp.float32
    owner = lax.axis_index("shard")
    steps = jnp.full((1, CO), step_count[0], jnp.int32).astype(f32)
    aux[0:1, :] = 1.0 - jnp.exp(-decay_power * jnp.log(steps))
    aux[1:3, :] = col_moment[...]
    aux[3:8, :] = jnp.zeros((5, CO), f32)
    for i in range(OWN):
        flag = jnp.where(order[owner * OWN + i] >= NB3, 1.0, 0.0).astype(f32)
        aux[8 + i : 9 + i, :] = jnp.full((1, CO), flag, f32)
    aux[15:16, :] = jnp.zeros((1, CO), f32)
    rows = OWN * BLK
    row_column[...] = jnp.sum(
        jnp.where(diagonal((rows, rows)), row_moment[...], 0.0), axis=1, keepdims=True
    )
    bf16 = jnp.bfloat16

    def note(block, outer_place, inner_place):
        outer[block] = outer_place
        inner[block] = inner_place

    each_stored_block(order, note)
    shift_columns(tiles, shifted)
    for part in range(4):
        rows = slice(128 * part, 128 * part + 128)
        values = pre[rows, :].astype(f32)
        sigma = jax.nn.sigmoid(values)
        act[rows, :] = (values * sigma).astype(bf16)
        cotangent = grad_out[rows, :]
        grad_act = lax.dot_general(
            cotangent, live[...], (((1,), (1,)), ((), ())), preferred_element_type=f32
        )
        grad_pre = grad_act * (sigma * (1.0 + values * (1.0 - sigma)))
        left[:, rows] = grad_pre.T.astype(bf16)
        right[:, rows] = cotangent.astype(f32).T.astype(bf16)

    def emit(first_block, product):
        result = product.T.astype(bf16)
        for j in range(8):
            block = first_block + j
            for q in range(4):
                row = 32 * j + 16 * (q // 2)
                lane = 128 * (q % 2)
                term[outer[block], q, inner[block]] = result[row : row + 16, lane : lane + 128]

    @pl.loop(0, 9, unroll=3)
    def _(spot):
        down, across = spot // 3, spot % 3
        for frame in range(3):
            window = shifted[across, frame : frame + FR, pl.ds(down, HW)].reshape(FR * HW * HW, CI)
            product = jnp.dot(left[...], window, preferred_element_type=f32)
            emit(8 * (9 * frame + spot), product)

    emit(NB3, jnp.dot(right[...], act[...], preferred_element_type=f32))


def backward(
    block_order,
    step_count,
    saved_tiles,
    pre_act,
    grad_output,
    pointwise_live,
    col_moment,
    row_moment,
):
    bf16 = jnp.bfloat16
    vmem = pl.BlockSpec(memory_space=pltpu.VMEM)
    smem = pl.BlockSpec(memory_space=pltpu.SMEM)
    return pl.pallas_call(
        backward_kernel,
        name="backward",
        out_shape=(
            jax.ShapeDtypeStruct((8, 4, 28, 16, 128), bf16),
            jax.ShapeDtypeStruct((16, CO), jnp.float32),
            jax.ShapeDtypeStruct((OWN * BLK, 1), jnp.float32),
        ),
        in_specs=[smem] * 2 + [vmem] * 6,
        out_specs=[vmem] * 3,
        scratch_shapes=[
            pltpu.VMEM((3, FR + 2, HW + 2, HW, CI), bf16),
            pltpu.VMEM((CO, FR * HW * HW), bf16),
            pltpu.VMEM((CO, FR * HW * HW), bf16),
            pltpu.VMEM((FR * HW * HW, CO), bf16),
            pltpu.SMEM((NB,), jnp.int32),
            pltpu.SMEM((NB,), jnp.int32),
        ],
        compiler_params=pltpu.CompilerParams(vmem_limit_bytes=VMEM_GRANT),
    )(
        block_order,
        step_count,
        saved_tiles,
        pre_act,
        grad_output,
        pointwise_live,
        col_moment,
        row_moment.reshape(1, OWN * BLK),
    )


def forward_kernel(
    order,
    shifted,
    gathered,
    update_in,
    master_in,
    row_in,
    col_in,
    output,
    update,
    master,
    new_row,
    new_col,
    kernels,
    hidden,
):
    f32 = jnp.float32
    rows = OWN * BLK
    new_row[...] = jnp.sum(
        jnp.where(diagonal((rows, rows)), row_in[...], 0.0), axis=0, keepdims=True
    )
    new_col[...] = col_in[0:2, :]
    update[...] = update_in[...]
    master[...] = master_in[...]

    def place(block, outer, inner):
        for q in range(4):
            lane = 128 * (q % 2)
            kernels[block, q // 2, :, lane : lane + 128] = gathered[outer, q, inner]

    each_stored_block(order, place)
    hidden[...] = jnp.zeros_like(hidden)

    @pl.loop(0, 9, unroll=3)
    def _(spot):
        down, across = spot // 3, spot % 3
        for frame in range(3):
            window = shifted[across, frame : frame + FR, pl.ds(down, HW)].reshape(FR * HW * HW, CI)
            matrix = kernels[pl.ds(8 * (9 * frame + spot), 8)].reshape(CI, CO)
            hidden[...] += jnp.dot(window, matrix, preferred_element_type=f32)

    pointwise = kernels[NB3:NB].reshape(CO, CO)
    for part in range(4):
        rows = slice(128 * part, 128 * part + 128)
        values = hidden[rows, :]
        acted = (values * jax.nn.sigmoid(values)).astype(jnp.bfloat16)
        output[rows, :] = jnp.dot(acted, pointwise, preferred_element_type=f32).astype(jnp.bfloat16)


def forward(block_order, shifted, gathered, update, master, row, col):
    bf16 = jnp.bfloat16
    f32 = jnp.float32
    vmem = pl.BlockSpec(memory_space=pltpu.VMEM)
    smem = pl.BlockSpec(memory_space=pltpu.SMEM)
    return pl.pallas_call(
        forward_kernel,
        name="forward",
        out_shape=(
            jax.ShapeDtypeStruct((FR * HW * HW, CO), bf16),
            jax.ShapeDtypeStruct(update.shape, f32),
            jax.ShapeDtypeStruct(master.shape, f32),
            jax.ShapeDtypeStruct((1, OWN * BLK), f32),
            jax.ShapeDtypeStruct((2, CO), f32),
        ),
        in_specs=[smem] + [vmem] * 6,
        out_specs=[vmem] * 5,
        scratch_shapes=[
            pltpu.VMEM((NB, 2, 16, CO), bf16),
            pltpu.VMEM((FR * HW * HW, CO), f32),
        ],
        compiler_params=pltpu.CompilerParams(vmem_limit_bytes=VMEM_GRANT),
    )(block_order, shifted, gathered, update, master, row, col)


def shards(
    step_count,
    block_order,
    saved_tiles,
    pre_act,
    grad_output,
    pointwise_live,
    master_rows,
    row_moment,
    col_moment,
    next_tiles,
):
    term, aux, row_column = backward(
        block_order,
        step_count,
        saved_tiles,
        pre_act,
        grad_output,
        pointwise_live,
        col_moment,
        row_moment,
    )
    term = term.reshape(2, 4, 4, 4, OWN, 16, 128)
    update, new_master, new_row, new_col, gathered, shifted = optimizer_step(
        term,
        aux,
        row_column.reshape(OWN, BLK, 1),
        master_rows.reshape(OWN, BLK, CO),
        next_tiles,
    )
    next_output, update, new_master, new_row, new_col = forward(
        block_order,
        shifted,
        gathered.reshape(8, 4, 28, 16, 128),
        update,
        new_master,
        new_row.reshape(OWN * BLK, 1),
        new_col,
    )
    return (
        update.reshape(master_rows.shape),
        new_master.reshape(master_rows.shape),
        new_row.reshape(row_moment.shape),
        new_col,
        next_output,
    )


def solution(mesh):
    in_specs = (
        P(),
        P(),
        P(("group", "shard"), None, None, None, None),
        P(("group", "shard"), None),
        P(("group", "shard"), None),
        P(),
        P("shard", None),
        P("shard"),
        P(),
        P(("group", "shard"), None, None, None, None),
    )
    out_specs = (P("shard", None), P("shard", None), P("shard"), P(), P(("group", "shard"), None))
    return jax.shard_map(shards, mesh=mesh, in_specs=in_specs, out_specs=out_specs, check_vma=False)
```
